256 devices in a mesh: seq: 32 (over z, y), head: 2 (over core), dp: 4 (over x).
Axes of the slice: x: 4, y: 4, z: 8, core: 2. Of those that a mesh axis runs over, the one named last changes fastest.
Arguments:
- series: bfloat16 [4, 16384, 768], P('dp', 'seq'), may hold values from -6 to 6
- norm_attn: float32 [768], replicated, may hold values from 0.1 to 1.9
- qkv_weight: bfloat16 [768, 3, 768], P(None, None, 'head'), may hold values from -0.21875 to 0.21875
- out_weight: bfloat16 [768, 768], P('head'), may hold values from -0.21875 to 0.21875
- norm_moe: float32 [768], replicated, may hold values from 0.1 to 1.9
- router_weight: bfloat16 [768, 128], replicated, may hold values from -0.21875 to 0.21875
- expert_ids: int32 [4, 16384, 1], P('dp', ('seq', 'head')), may hold values from 0 to 127; in each aligned block of 256 rows (0 to 255, 256 to 511, ..., all dimensions but the last counted through in order) at most 4 rows name the same one
- gate_weight: bfloat16 [128, 768, 3072], P(('seq', 'dp'), None, 'head'), may hold values from -0.21875 to 0.21875
- up_weight: bfloat16 [128, 768, 3072], P(('seq', 'dp'), None, 'head'), may hold values from -0.21875 to 0.21875
- down_weight: bfloat16 [128, 3072, 768], P(('seq', 'dp'), 'head'), may hold values from -0.109375 to 0.109375
Outputs:
- layer_out: bfloat16 [4, 16384, 768], P('dp', ('seq', 'head'))
The draws below stay inside these ranges and needn't reach their ends.
Inputs may be any that keep to these rules, and one draw needn't show every extreme that they name: `expert_ids`: among the rows of one device (aligned blocks of 256 positions, counted over series and positions in order) at most 4 name the same expert, and in every draw some expert is named by exactly 4 rows of some device.
All inputs are finite; a program needn't handle non-finite values.
Results may differ from the reference program's by a relative error of at most 0.0041.
Values may be sent and summed in bfloat16 or wider, within the bound.
No kernel may reach another device: no remote copies, remote signals or barrier semaphores. Data moves between devices by JAX's collectives and lax.ppermute only.
A program may use at most 128 MiB of HBM per device.

```python
import math
import jax
import jax.numpy as jnp
import numpy as np
from jax import lax

D = 768
HEADS = 6
HD = 128
FF = 3072
BLOCK = 512
BATCH = 4
LEN = 16384
EXPERTS = 128
ROWS_DEV = 256
CAP = 4


def draw_series(key, part):
    first_key, second_key = jax.random.split(key, 2)
    segment_count = LEN // 128
    noise_part = jax.random.normal(first_key, (BATCH, LEN, D), jnp.float32)
    offsets = jax.random.normal(second_key, (BATCH, segment_count, D), jnp.float32)
    values = 0.7 * (noise_part + jnp.repeat(offsets, 128, axis=1))
    return jnp.clip(values, -6.0, 6.0).astype(jnp.bfloat16)


def steps_of(stream_key, extent, pieces, low, largest):
    level = 1.0
    for dim, parts in pieces:
        draws = jax.random.uniform(jax.random.fold_in(jax.random.fold_in(stream_key, 6), dim), (parts,), jnp.float32, low / len(pieces), largest / len(pieces))
        level = level * jnp.repeat(jnp.exp(draws), extent[dim] // parts).reshape((-1,) + (1,) * (len(extent) - 1 - dim))
    return level


def deal_out(rng, own, number, rows, count, top, most, skew):
    order = jax.random.permutation(rng, count)
    heavy_load, ordinary = portions_of(count, rows * top, most, skew, True), portions_of(count, rows * top, most, skew, False)
    places = jnp.arange(count)

    def named(tallies, offset_by):
        used = int((tallies > 0).sum())
        fixed = max(1, used // 4)
        passed = fixed + (places - fixed + offset_by * (used - fixed)) % max(1, count - fixed)
        return jnp.zeros((count,), jnp.int32).at[order[jnp.where(places < fixed, places, passed)]].set(jnp.asarray(tallies, jnp.int32))

    tallies = jnp.where(number % 4 == 0, named(heavy_load, number // 4), named(ordinary, number - number // 4 - 1))
    mixed = jax.random.permutation(jax.random.fold_in(own, 3), count)
    source_of, receiver = mixed[0:count // 2 * 2:2], mixed[1:count // 2 * 2:2]
    room = jnp.minimum(tallies[source_of] - 1, most - tallies[receiver]) // 2
    room = jnp.where((source_of == order[0]) | (receiver == order[0]) | (tallies[receiver] == 0), 0, jnp.maximum(room, 0))
    passed = jax.random.randint(jax.random.fold_in(own, 4), (count // 2,), 0, 1 << 20) % (room + 1)
    tallies = tallies.at[source_of].add(-passed).at[receiver].add(passed)
    items = jnp.searchsorted(jnp.cumsum(tallies), jnp.arange(rows * top), side="right").astype(jnp.int32)
    listing = items.reshape(top, rows).T
    listing = listing[jax.random.permutation(jax.random.fold_in(own, 1), rows)]
    offset_by = jax.random.randint(jax.random.fold_in(own, 2), (rows, 1), 0, top)
    return jnp.take_along_axis(listing, (jnp.arange(top)[None, :] + offset_by) % top, axis=1)


def portions_of(count, total, bound, lean, full):
    loads = [(1 << 20) // math.isqrt(rank ** lean) + 1 for rank in range(1, count + 1)]
    largest = bound if full else min(bound, max(-(-total // count), total * loads[0] // sum(loads)))
    least = 1 if total - largest >= count - 1 else 0
    given, rest = [largest] + [least] * (count - 1), total - largest - least * (count - 1)
    while rest > 0:
        free = [i for i in range(1, count) if given[i] < largest] or [i for i in range(1, count) if given[i] < bound]
        pool, left = sum([loads[i] for i in free]), rest
        for i in free:
            addition = min(bound - given[i], max(1, left * loads[i] // pool), rest)
            given[i] = given[i] + addition
            rest = rest - addition
    return np.array(given)


def gaussian(key, shape, spread, reach, pieces=(), held_as=jnp.bfloat16):
    result = jax.random.normal(key, shape, jnp.float32) * spread
    if len(pieces) > 0:
        result = steps_of(key, shape, pieces, -0.22, 0.18) * result
    return jnp.clip(result, min=-reach, max=reach).astype(held_as)


def setup_inputs(seed: int = 0) -> dict:
    streams_of = jax.random.split(jax.random.key(seed), 11)
    series = draw_series(jax.random.fold_in(streams_of[10], 71), 0)
    norm_attn = jnp.clip(1.0 + 0.18 * jax.random.normal(streams_of[1], (D,), jnp.float32), 0.1, 1.9)
    qkv_weight = gaussian(streams_of[2], (D, 3, HEADS * HD), D ** -0.5, 0.21875, ((2, 2),))
    out_weight = gaussian(streams_of[3], (HEADS * HD, D), (HEADS * HD) ** -0.5, 0.21875, ((0, 2),))
    norm_moe = jnp.clip(1.0 + 0.18 * jax.random.normal(streams_of[4], (D,), jnp.float32), 0.1, 1.9)
    router_weight = gaussian(streams_of[5], (D, EXPERTS), D ** -0.5, 0.21875)
    expert_ids_keys = jax.random.split(jax.random.fold_in(streams_of[6], 1), BATCH * LEN // ROWS_DEV)
    expert_ids_turns = jax.random.permutation(jax.random.fold_in(streams_of[6], 3), BATCH * LEN // ROWS_DEV)
    expert_ids = jax.vmap(lambda own, number: deal_out(jax.random.fold_in(streams_of[6], 2), own, number, ROWS_DEV, EXPERTS, 1, CAP, 2))(expert_ids_keys, expert_ids_turns).reshape((BATCH, LEN, 1))
    gate_weight = gaussian(streams_of[7], (EXPERTS, D, FF), D ** -0.5, 0.21875, ((0, 128), (2, 2)))
    up_weight = gaussian(streams_of[8], (EXPERTS, D, FF), D ** -0.5, 0.21875, ((0, 128), (2, 2)))
    down_weight = gaussian(streams_of[9], (EXPERTS, FF, D), FF ** -0.5, 0.109375, ((0, 128), (1, 2)))
    return dict(series=series, norm_attn=norm_attn, qkv_weight=qkv_weight, out_weight=out_weight, norm_moe=norm_moe, router_weight=router_weight, expert_ids=expert_ids, gate_weight=gate_weight, up_weight=up_weight, down_weight=down_weight)


NORM_EPS = 1e-06

def rms_scale(values, gain):
    values = values.astype(jnp.float32)
    return values * lax.rsqrt(lax.optimization_barrier(jnp.mean(values * values, axis=-1, keepdims=True)) + NORM_EPS) * gain

def attend_series(queries, key_rows, value_rows):
    block_count = LEN // BLOCK
    query_blocks = queries.reshape(block_count, BLOCK, HEADS, HD)
    key_blocks = key_rows.reshape(block_count, BLOCK, HEADS, HD)
    value_blocks = value_rows.reshape(block_count, BLOCK, HEADS, HD)
    causal = jnp.arange(BLOCK)[:, None] >= jnp.arange(BLOCK)[None, :]

    def block_step(kv_state, inputs):
        query_part, key_part, value_part = inputs
        query_f = query_part.astype(jnp.float32)
        key_f = key_part.astype(jnp.float32)
        value_f = value_part.astype(jnp.float32)
        scores = jnp.einsum('qhd,khd->hqk', query_f, key_f, precision=lax.Precision.HIGHEST)
        scores = jnp.where(causal[None], scores, 0.0)
        scores = lax.optimization_barrier(scores.astype(jnp.bfloat16)).astype(jnp.float32)
        inside = jnp.einsum('hqk,khd->qhd', scores, value_f, precision=lax.Precision.HIGHEST)
        carried = jnp.einsum('qhd,hde->qhe', query_f, kv_state, precision=lax.Precision.HIGHEST)
        kv_state = kv_state + jnp.einsum('khd,khe->hde', key_f, value_f, precision=lax.Precision.HIGHEST)
        return (kv_state, inside + carried)
    initial = jnp.zeros((HEADS, HD, HD), jnp.float32)
    _, mixed_heads = lax.scan(block_step, initial, (query_blocks, key_blocks, value_blocks))
    return mixed_heads.reshape(LEN, HEADS, HD)

def reference(series, norm_attn, qkv_weight, out_weight, norm_moe, router_weight, expert_ids, gate_weight, up_weight, down_weight):
    total_rows = BATCH * LEN
    normed_in = rms_scale(series, norm_attn).astype(jnp.bfloat16)
    projected = jnp.dot(normed_in.reshape(total_rows, D), qkv_weight.reshape(D, 3 * HEADS * HD), preferred_element_type=jnp.float32).astype(jnp.bfloat16)
    projected = projected.reshape(BATCH, LEN, 3, HEADS, HD)
    position_scale = (jnp.arange(LEN).astype(jnp.float32) + 1.0) * jnp.sqrt(jnp.float32(HD))

    def one_series(qkv_parts):
        mixed_heads = attend_series(qkv_parts[:, 0], qkv_parts[:, 1], qkv_parts[:, 2])
        return (mixed_heads / position_scale[:, None, None]).astype(jnp.bfloat16)
    heads_out = lax.map(one_series, projected)
    attention = jnp.dot(heads_out.reshape(total_rows, HEADS * HD), out_weight, preferred_element_type=jnp.float32)
    residual = series.reshape(total_rows, D).astype(jnp.float32) + attention
    normed_moe = rms_scale(residual, norm_moe).astype(jnp.bfloat16)
    route_ids = expert_ids.reshape(total_rows).astype(jnp.int32)
    logits = jnp.dot(normed_moe, router_weight, preferred_element_type=jnp.float32)
    gate_value = jax.nn.sigmoid(jnp.take_along_axis(logits, route_ids[:, None], axis=1))
    slot_most = total_rows // ROWS_DEV * CAP
    sort_order = jnp.argsort(route_ids, stable=True).astype(jnp.int32)
    counts = jnp.zeros((EXPERTS,), jnp.int32).at[route_ids].add(1).astype(jnp.int32)
    starts = (jnp.cumsum(counts) - counts).astype(jnp.int32)
    slots = jnp.arange(slot_most).astype(jnp.int32)

    def one_expert(expert_index):
        place = jnp.clip(starts[expert_index] + slots, 0, total_rows - 1).astype(jnp.int32)
        source = sort_order[place]
        picked_rows = normed_moe[source]
        gate_proj = jnp.dot(picked_rows, gate_weight[expert_index], preferred_element_type=jnp.float32)
        up_proj = jnp.dot(picked_rows, up_weight[expert_index], preferred_element_type=jnp.float32)
        hidden = (jax.nn.silu(gate_proj) * up_proj).astype(jnp.bfloat16)
        expert_out = jnp.dot(hidden, down_weight[expert_index], preferred_element_type=jnp.float32).astype(jnp.bfloat16)
        live_slot = slots < counts[expert_index]
        return (jnp.where(live_slot[:, None], expert_out, jnp.zeros_like(expert_out)), source)
    expert_outs, sources = lax.map(one_expert, jnp.arange(EXPERTS).astype(jnp.int32))
    routed = jnp.zeros((total_rows, D), jnp.float32).at[sources.reshape(-1)].add(expert_outs.reshape(-1, D).astype(jnp.float32))
    layer_out = (residual + gate_value * routed).astype(jnp.bfloat16)
    return layer_out.reshape(BATCH, LEN, D)
```

```python
import jax
import jax.numpy as jnp
from jax import lax
from jax.experimental import pallas as pl
from jax.experimental.pallas import tpu as pltpu
from jax.sharding import Mesh
from jax.sharding import PartitionSpec as P

HD = 128
BLOCK = 512
SEQ = ("seq_0", "seq_1")
SEQ_DP = ("seq_0", "seq_1", "dp")
SEQ_HEAD = ("seq_0", "seq_1", "head")
NORM_EPS = 1e-06
FF_BLOCK = 512


def rms_scale(values, gain):
    values = values.astype(jnp.float32)
    return values * lax.rsqrt(jnp.mean(values * values, axis=-1, keepdims=True) + NORM_EPS) * gain


def from_partner(shard):
    return lax.ppermute(shard, "head", [(0, 1), (1, 0)])


def exchange(pieces, axes):
    return lax.all_to_all(pieces, axes, split_axis=0, concat_axis=0, tiled=True)


def expert_kernel(blocks, rows, gate_a, up_a, down_a, gate_b, up_b, down_b, out, total):
    step = pl.program_id(0)

    def add_part(gate, up, down):
        x = rows[...]
        g = jnp.dot(x, gate[...], preferred_element_type=jnp.float32)
        u = jnp.dot(x, up[...], preferred_element_type=jnp.float32)
        hidden = (g / (1.0 + jnp.exp(-g)) * u).astype(jnp.bfloat16)
        return jnp.dot(hidden, down[...], preferred_element_type=jnp.float32)

    @pl.when(step == 0)
    def _():
        total[...] = add_part(gate_a, up_a, down_a)

    @pl.when(jnp.logical_and(step > 0, step < blocks))
    def _():
        total[...] += add_part(gate_a, up_a, down_a)

    @pl.when(step >= blocks)
    def _():
        total[...] += add_part(gate_b, up_b, down_b)

    @pl.when(step == 2 * blocks - 1)
    def _():
        out[...] = total[...].astype(out.dtype)


def expert_of(rows, own, partner):
    count, width = rows.shape
    units = own[0].shape[1]
    blocks = units // FF_BLOCK

    def first(step):
        return jnp.minimum(step, blocks - 1)

    def second(step):
        return jnp.maximum(step - blocks, 0)

    def specs(place):
        return [
            pl.BlockSpec((width, FF_BLOCK), lambda i: (0, place(i))),
            pl.BlockSpec((width, FF_BLOCK), lambda i: (0, place(i))),
            pl.BlockSpec((FF_BLOCK, width), lambda i: (place(i), 0)),
        ]

    return pl.pallas_call(
        lambda *refs: expert_kernel(blocks, *refs),
        grid=(2 * blocks,),
        in_specs=[pl.BlockSpec((count, width), lambda i: (0, 0))] + specs(first) + specs(second),
        out_specs=pl.BlockSpec((count, width), lambda i: (0, 0)),
        out_shape=jax.ShapeDtypeStruct((count, width), jnp.bfloat16),
        scratch_shapes=[pltpu.VMEM((count, width), jnp.float32)],
        compiler_params=pltpu.CompilerParams(
            dimension_semantics=("arbitrary",), vmem_limit_bytes=48 * 1024 * 1024
        ),
        cost_estimate=pl.CostEstimate(
            flops=2 * count * width * units * 6,
            bytes_accessed=12 * width * units,
            transcendentals=2 * count * units,
        ),
        name="expert_mlp",
    )(rows, *own, *partner)


def on_device(
    series,
    norm_attn,
    qkv_weight,
    out_weight,
    norm_moe,
    router_weight,
    expert_ids,
    gate_weight,
    up_weight,
    down_weight,
):
    rows_all = series.shape[1]
    width = series.shape[2]
    head_count = lax.axis_size("head")
    half = qkv_weight.shape[2]
    heads = half // HD
    own_rows = rows_all // head_count
    head_rank = lax.axis_index("head")
    seq_rank = lax.axis_index(SEQ)
    seq_size = lax.axis_size(SEQ)

    qkv_other = from_partner(qkv_weight)
    out_other = from_partner(out_weight)
    own_expert = (gate_weight[0], up_weight[0], down_weight[0])
    other_expert = tuple(from_partner(w) for w in own_expert)

    normed_in = rms_scale(series[0], norm_attn).astype(jnp.bfloat16)
    kv_own = jnp.dot(
        normed_in, qkv_weight[:, 1:].reshape(width, 2 * half), preferred_element_type=jnp.float32
    ).astype(jnp.bfloat16)
    keys_own, values_own = kv_own[:, :half], kv_own[:, half:]
    state = jnp.concatenate(
        [
            lax.dot_general(
                keys_own[:, n * HD : (n + 1) * HD],
                values_own[:, n * HD : (n + 1) * HD],
                (((0,), (0,)), ((), ())),
                preferred_element_type=jnp.float32,
            )
            for n in range(heads)
        ],
        axis=1,
    ).astype(jnp.bfloat16)
    lines = HD // seq_size
    pieces = exchange(state.reshape(seq_size, lines, half), SEQ)
    earlier = (jnp.arange(seq_size)[:, None] > jnp.arange(seq_size)[None, :]).astype(jnp.float32)
    before = lax.dot_general(
        earlier,
        pieces.astype(jnp.float32),
        (((1,), (0,)), ((), ())),
        precision=lax.Precision.HIGHEST,
        preferred_element_type=jnp.float32,
    ).astype(jnp.bfloat16)
    before = jnp.broadcast_to(before[:, None], (seq_size, head_count, lines, half))
    states = exchange(before.reshape(seq_size * head_count, lines, half), SEQ_HEAD)
    states = jnp.moveaxis(states.reshape(seq_size, head_count, lines, half), 1, 0)
    states = states.reshape(head_count, HD, half)
    state_own = jnp.where(head_rank == 0, states[0], states[1])
    state_other = jnp.where(head_rank == 0, states[1], states[0])

    first_row = head_rank * own_rows
    normed_own = lax.dynamic_slice_in_dim(normed_in, first_row, own_rows, 0)
    kv_other = jnp.dot(
        normed_in, qkv_other[:, 1:].reshape(width, 2 * half), preferred_element_type=jnp.float32
    ).astype(jnp.bfloat16)
    block_row = first_row + jnp.arange(own_rows)
    causal = block_row[:, None] >= jnp.arange(rows_all)[None, :]
    position = (seq_rank * rows_all + block_row + 1).astype(jnp.float32)
    scale = (position * jnp.sqrt(jnp.float32(HD)))[:, None]

    def attend(weight, kv, start_state):
        queries = jnp.dot(normed_own, weight[:, 0], preferred_element_type=jnp.float32).astype(
            jnp.bfloat16
        )
        mixed = []
        for n in range(heads):
            at = slice(n * HD, (n + 1) * HD)
            scores = lax.dot_general(
                queries[:, at],
                kv[:, :half][:, at],
                (((1,), (1,)), ((), ())),
                preferred_element_type=jnp.float32,
            )
            scores = jnp.where(causal, scores, 0.0).astype(jnp.bfloat16)
            inside = jnp.dot(scores, kv[:, half:][:, at], preferred_element_type=jnp.float32)
            carried = jnp.dot(
                queries[:, at], start_state[:, at], preferred_element_type=jnp.float32
            )
            mixed.append(((inside + carried) / scale).astype(jnp.bfloat16))
        return jnp.concatenate(mixed, axis=1)

    mixed_own = attend(qkv_weight, kv_own, state_own)
    mixed_other = attend(qkv_other, kv_other, state_other)
    attention = jnp.dot(mixed_own, out_weight, preferred_element_type=jnp.float32) + jnp.dot(
        mixed_other, out_other, preferred_element_type=jnp.float32
    )
    own_series = lax.dynamic_slice_in_dim(series[0], first_row, own_rows, 0).astype(jnp.float32)
    residual = own_series + attention
    normed_moe = rms_scale(residual, norm_moe).astype(jnp.bfloat16)

    route_ids = expert_ids[0, :, 0]
    expert_count = router_weight.shape[1]
    capacity = 2 * own_rows // expert_count
    logits = jnp.dot(normed_moe, router_weight, preferred_element_type=jnp.float32)
    picked_expert = route_ids[:, None] == jnp.arange(expert_count, dtype=jnp.int32)[None, :]
    gate_value = jax.nn.sigmoid(
        jnp.sum(jnp.where(picked_expert, logits, 0.0), axis=1, keepdims=True)
    )
    earlier_row = jnp.arange(own_rows)[None, :] < jnp.arange(own_rows)[:, None]
    same_expert = route_ids[:, None] == route_ids[None, :]
    slot_rank = jnp.sum(jnp.logical_and(same_expert, earlier_row), axis=1)
    slot_index = route_ids * capacity + slot_rank
    routing = (
        slot_index[:, None] == jnp.arange(expert_count * capacity, dtype=jnp.int32)[None, :]
    ).astype(jnp.bfloat16)
    send_buffer = lax.dot_general(
        routing, normed_moe, (((0,), (0,)), ((), ())), preferred_element_type=jnp.float32
    )
    send_buffer = send_buffer.astype(jnp.bfloat16).reshape(expert_count, capacity, width)
    received = exchange(send_buffer, SEQ_DP)
    expert_out = expert_of(received.reshape(-1, width), own_expert, other_expert)
    returned = exchange(expert_out.reshape(received.shape), SEQ_DP)
    routed = jnp.dot(
        routing,
        returned.reshape(expert_count * capacity, width),
        preferred_element_type=jnp.float32,
    )
    layer_out = (residual + gate_value * routed).astype(jnp.bfloat16)
    return layer_out[None]


def solution(mesh):
    split = Mesh(
        mesh.devices.reshape(8, 4, mesh.shape["head"], mesh.shape["dp"]),
        ("seq_0", "seq_1", "head", "dp"),
    )
    placed = (
        P("dp", SEQ, None),
        P(),
        P(None, None, "head"),
        P("head", None),
        P(),
        P(),
        P("dp", SEQ_HEAD, None),
        P(SEQ_DP, None, "head"),
        P(SEQ_DP, None, "head"),
        P(SEQ_DP, "head", None),
    )
    return jax.shard_map(
        on_device, mesh=split, in_specs=placed, out_specs=P("dp", SEQ_HEAD, None), check_vma=False
    )
```

```python
import math

import jax
import jax.numpy as jnp
from jax import lax
from jax.experimental import pallas as pl
from jax.experimental.pallas import tpu as pltpu
from jax.sharding import Mesh
from jax.sharding import PartitionSpec as P

HD = 128
BLOCK = 512
SEQ = ("seq_0", "seq_1")
SEQ_DP = ("seq_0", "seq_1", "dp")
SEQ_HEAD = ("seq_0", "seq_1", "head")
NORM_EPS = 1e-06
FF_BLOCK = 512
MIB = 1024 * 1024


def from_partner(shard):
    return lax.ppermute(shard, "head", [(0, 1), (1, 0)])


def exchange(pieces, axes):
    return lax.all_to_all(pieces, axes, split_axis=0, concat_axis=0, tiled=True)


def expert_kernel(blocks, rows, gate_a, up_a, down_a, gate_b, up_b, down_b, out, total):
    step = pl.program_id(0)

    def add_part(gate, up, down):
        x = rows[...]
        g = jnp.dot(x, gate[...], preferred_element_type=jnp.float32)
        u = jnp.dot(x, up[...], preferred_element_type=jnp.float32)
        hidden = (g * (0.5 + 0.5 * jnp.tanh(0.5 * g)) * u).astype(jnp.bfloat16)
        return jnp.dot(hidden, down[...], preferred_element_type=jnp.float32)

    @pl.when(step == 0)
    def _():
        total[...] = add_part(gate_a, up_a, down_a)

    @pl.when(jnp.logical_and(step > 0, step < blocks))
    def _():
        total[...] += add_part(gate_a, up_a, down_a)

    @pl.when(step >= blocks)
    def _():
        total[...] += add_part(gate_b, up_b, down_b)

    @pl.when(step == 2 * blocks - 1)
    def _():
        out[...] = total[...].astype(out.dtype)


def expert_of(rows, own, partner):
    count, width = rows.shape
    units = own[0].shape[1]
    blocks = units // FF_BLOCK

    def first(step):
        return jnp.minimum(step, blocks - 1)

    def second(step):
        return jnp.maximum(step - blocks, 0)

    def specs(place):
        return [
            pl.BlockSpec((width, FF_BLOCK), lambda i: (0, place(i))),
            pl.BlockSpec((width, FF_BLOCK), lambda i: (0, place(i))),
            pl.BlockSpec((FF_BLOCK, width), lambda i: (place(i), 0)),
        ]

    return pl.pallas_call(
        lambda *refs: expert_kernel(blocks, *refs),
        grid=(2 * blocks,),
        in_specs=[pl.BlockSpec((count, width), lambda i: (0, 0))] + specs(first) + specs(second),
        out_specs=pl.BlockSpec((count, width), lambda i: (0, 0)),
        out_shape=jax.ShapeDtypeStruct((count, width), jnp.bfloat16),
        scratch_shapes=[pltpu.VMEM((count, width), jnp.float32)],
        compiler_params=pltpu.CompilerParams(
            dimension_semantics=("arbitrary",), vmem_limit_bytes=32 * MIB
        ),
        cost_estimate=pl.CostEstimate(
            flops=2 * count * width * units * 6,
            bytes_accessed=12 * width * units,
            transcendentals=2 * count * units,
        ),
        name="expert_mlp",
    )(rows, *(in_hbm(w) for w in own), *(in_hbm(w) for w in partner))


def in_hbm(array):
    return pltpu.with_memory_space_constraint(array, pltpu.HBM)


def normed_rows(rows, gain):
    x = rows.astype(jnp.float32)
    mean = jnp.sum(x * x, axis=-1, keepdims=True) * (1.0 / x.shape[1])
    return x * lax.rsqrt(mean + NORM_EPS) * gain


def state_kernel(series, weight, gain, state_out, rows, table, sems):
    half = table.shape[2]
    fetch_rows = pltpu.make_async_copy(series, rows, sems.at[0])
    fetch_keys = pltpu.make_async_copy(weight.at[1], table.at[0], sems.at[1])
    fetch_values = pltpu.make_async_copy(weight.at[2], table.at[1], sems.at[2])
    fetch_rows.start()
    fetch_keys.start()
    fetch_values.start()
    fetch_rows.wait()
    normed = normed_rows(rows[...], gain[...]).astype(jnp.bfloat16)
    fetch_keys.wait()
    keys = jnp.dot(normed, table[0], preferred_element_type=jnp.float32).astype(jnp.bfloat16)
    fetch_values.wait()
    values = jnp.dot(normed, table[1], preferred_element_type=jnp.float32).astype(jnp.bfloat16)
    heads = half // HD
    for n in range(heads):
        at = slice(n * HD, (n + 1) * HD)
        state_out[at, :] = lax.dot_general(
            keys[:, at], values[:, at], (((0,), (0,)), ((), ())), preferred_element_type=jnp.float32
        ).astype(jnp.bfloat16)
    state_out[heads * HD :, :] = jnp.zeros((HD, HD), jnp.bfloat16)


def block_state(series, weight, gain):
    count, width = series.shape
    half = weight.shape[2]
    return pl.pallas_call(
        state_kernel,
        in_specs=[
            pl.BlockSpec(memory_space=pl.ANY),
            pl.BlockSpec(memory_space=pl.ANY),
            pl.BlockSpec(memory_space=pltpu.VMEM),
        ],
        out_specs=pl.BlockSpec(memory_space=pltpu.VMEM),
        out_shape=jax.ShapeDtypeStruct((half + HD, HD), jnp.bfloat16),
        scratch_shapes=[
            pltpu.VMEM((count, width), jnp.bfloat16),
            pltpu.VMEM((2, width, half), jnp.bfloat16),
            pltpu.SemaphoreType.DMA((3,)),
        ],
        compiler_params=pltpu.CompilerParams(vmem_limit_bytes=24 * MIB),
        cost_estimate=pl.CostEstimate(
            flops=4 * count * width * half, bytes_accessed=4 * count * width, transcendentals=count
        ),
        name="block_state",
    )(in_hbm(series), in_hbm(weight), gain)


def prefix_kernel(pieces, out):
    total = jnp.zeros(pieces.shape[1:], jnp.float32)
    for k in range(pieces.shape[0]):
        rounded = total.astype(jnp.bfloat16)
        out[k, 0] = rounded
        out[k, 1] = rounded
        total = total + pieces[k].astype(jnp.float32)


def prefix(pieces):
    count, lines, lanes = pieces.shape
    return pl.pallas_call(
        prefix_kernel,
        in_specs=[pl.BlockSpec(memory_space=pltpu.VMEM)],
        out_specs=pl.BlockSpec(memory_space=pltpu.VMEM),
        out_shape=jax.ShapeDtypeStruct((count, 2, lines, lanes), jnp.bfloat16),
        compiler_params=pltpu.CompilerParams(vmem_limit_bytes=4 * MIB),
        cost_estimate=pl.CostEstimate(
            flops=count * lines * lanes, bytes_accessed=6 * count * lines * lanes, transcendentals=0
        ),
        name="prefix",
    )(pieces)


def inside_kernel(series, gain, w_own, w_other, queries_out, inside_out):
    count, _ = series.shape
    own_rows = queries_out.shape[0]
    half = w_own.shape[2]
    heads = half // HD
    first_row = pl.multiple_of(lax.axis_index("head") * own_rows, own_rows)
    mine = normed_rows(series[pl.ds(first_row, own_rows), :], gain[...]).astype(jnp.bfloat16)
    normed = normed_rows(series[...], gain[...]).astype(jnp.bfloat16)
    row = lax.broadcasted_iota(jnp.int32, (own_rows, count), 0) + first_row
    causal = row >= lax.broadcasted_iota(jnp.int32, (own_rows, count), 1)
    for part, weight in ((0, w_own), (1, w_other)):
        queries, keys, values = (
            jnp.dot(rows, weight[k], preferred_element_type=jnp.float32).astype(jnp.bfloat16)
            for k, rows in ((0, mine), (1, normed), (2, normed))
        )
        queries_out[:, part * half : (part + 1) * half] = queries
        for n in range(heads):
            at = slice(n * HD, (n + 1) * HD)
            scores = lax.dot_general(
                queries[:, at],
                keys[:, at],
                (((1,), (1,)), ((), ())),
                preferred_element_type=jnp.float32,
            )
            scores = jnp.where(causal, scores, 0.0).astype(jnp.bfloat16)
            lanes = slice(part * half + n * HD, part * half + (n + 1) * HD)
            inside_out[:, lanes] = jnp.dot(
                scores, values[:, at], preferred_element_type=jnp.float32
            )


def inside_block(series, gain, w_own, w_other, own_rows):
    count, width = series.shape
    half = w_own.shape[2]
    return pl.pallas_call(
        inside_kernel,
        in_specs=[pl.BlockSpec(memory_space=pltpu.VMEM)] * 4,
        out_specs=[pl.BlockSpec(memory_space=pltpu.VMEM)] * 2,
        out_shape=[
            jax.ShapeDtypeStruct((own_rows, 2 * half), jnp.bfloat16),
            jax.ShapeDtypeStruct((own_rows, 2 * half), jnp.float32),
        ],
        compiler_params=pltpu.CompilerParams(vmem_limit_bytes=24 * MIB),
        cost_estimate=pl.CostEstimate(
            flops=10 * count * width * half + 8 * own_rows * count * half,
            bytes_accessed=8 * count * width,
            transcendentals=0,
        ),
        name="inside_block",
    )(series, gain, w_own, w_other)


def mix_kernel(
    queries,
    inside,
    states,
    out_own,
    out_other,
    series,
    gain,
    slots,
    residual_out,
    normed_out,
    send_out,
    queries_in,
    inside_in,
    weights_in,
    rows_in,
    residual_held,
    normed_held,
    sems,
):
    own_rows, width = rows_in.shape
    half = out_own.shape[0]
    heads = half // HD
    head_rank = lax.axis_index("head")
    first_row = pl.multiple_of(head_rank * own_rows, own_rows)
    fetches = [
        pltpu.make_async_copy(queries, queries_in, sems.at[0]),
        pltpu.make_async_copy(inside, inside_in, sems.at[1]),
        pltpu.make_async_copy(out_own, weights_in.at[0], sems.at[2]),
        pltpu.make_async_copy(out_other, weights_in.at[1], sems.at[3]),
        pltpu.make_async_copy(series.at[pl.ds(first_row, own_rows)], rows_in, sems.at[4]),
    ]
    for fetch in fetches:
        fetch.start()
    base = lax.axis_index(SEQ) * series.shape[0] + first_row + 1
    position = lax.broadcasted_iota(jnp.int32, (own_rows, HD), 0) + base
    unit = 1.0 / (position.astype(jnp.float32) * math.sqrt(HD))
    slot = lax.broadcasted_iota(jnp.int32, (send_out.shape[0], own_rows), 0)
    chosen = jnp.where(slot == slots[...], 1.0, 0.0).astype(jnp.bfloat16)
    per_head = HD // states.shape[2]
    fetches[0].wait()
    fetches[1].wait()
    mixed = []
    for part in range(2):
        rank = head_rank if part == 0 else 1 - head_rank
        for n in range(heads):
            lanes = slice(part * half + n * HD, part * half + (n + 1) * HD)
            start = states[n * per_head : (n + 1) * per_head, rank].reshape(HD, HD)
            carried = jnp.dot(queries_in[:, lanes], start, preferred_element_type=jnp.float32)
            mixed.append(((inside_in[:, lanes] + carried) * unit).astype(jnp.bfloat16))
    fetches[2].wait()
    total = jnp.dot(
        jnp.concatenate(mixed[:heads], axis=1), weights_in[0], preferred_element_type=jnp.float32
    )
    fetches[3].wait()
    total += jnp.dot(
        jnp.concatenate(mixed[heads:], axis=1), weights_in[1], preferred_element_type=jnp.float32
    )
    fetches[4].wait()
    total += rows_in[...].astype(jnp.float32)
    residual_held[...] = total
    keep_residual = pltpu.make_async_copy(residual_held, residual_out, sems.at[5])
    keep_residual.start()
    normed = normed_rows(total, gain[...]).astype(jnp.bfloat16)
    normed_held[...] = normed
    keep_normed = pltpu.make_async_copy(normed_held, normed_out, sems.at[6])
    keep_normed.start()
    send_out[...] = jnp.dot(chosen, normed, preferred_element_type=jnp.float32).astype(
        jnp.bfloat16
    )
    keep_residual.wait()
    keep_normed.wait()


def mix_heads(queries, inside, states, out_own, out_other, series, gain, slots, slot_count):
    own_rows, width = queries.shape
    half = out_own.shape[0]
    anywhere = pl.BlockSpec(memory_space=pl.ANY)
    local = pl.BlockSpec(memory_space=pltpu.VMEM)
    return pl.pallas_call(
        mix_kernel,
        in_specs=[anywhere, anywhere, local, anywhere, anywhere, anywhere, local, local],
        out_specs=[anywhere, anywhere, local],
        out_shape=[
            pltpu.HBM((own_rows, width), jnp.float32),
            pltpu.HBM((own_rows, width), jnp.bfloat16),
            jax.ShapeDtypeStruct((slot_count, width), jnp.bfloat16),
        ],
        scratch_shapes=[
            pltpu.VMEM((own_rows, width), jnp.bfloat16),
            pltpu.VMEM((own_rows, width), jnp.float32),
            pltpu.VMEM((2, half, width), jnp.bfloat16),
            pltpu.VMEM((own_rows, width), jnp.bfloat16),
            pltpu.VMEM((own_rows, width), jnp.float32),
            pltpu.VMEM((own_rows, width), jnp.bfloat16),
            pltpu.SemaphoreType.DMA((7,)),
        ],
        compiler_params=pltpu.CompilerParams(vmem_limit_bytes=24 * MIB),
        cost_estimate=pl.CostEstimate(
            flops=2 * own_rows * width * (width + HD + slot_count),
            bytes_accessed=12 * own_rows * width,
            transcendentals=own_rows,
        ),
        name="mix_heads",
    )(
        in_hbm(queries),
        in_hbm(inside),
        states,
        in_hbm(out_own),
        in_hbm(out_other),
        in_hbm(series),
        gain,
        slots,
    )


def on_device(
    series,
    norm_attn,
    qkv_weight,
    out_weight,
    norm_moe,
    router_weight,
    expert_ids,
    gate_weight,
    up_weight,
    down_weight,
):
    width = series.shape[2]
    head_count = lax.axis_size("head")
    seq_size = lax.axis_size(SEQ)
    own_rows = series.shape[1] // head_count

    qkv_own = jnp.moveaxis(qkv_weight, 1, 0)
    qkv_other = from_partner(qkv_own)
    out_other = from_partner(out_weight)
    own_expert = (gate_weight[0], up_weight[0], down_weight[0])
    other_expert = tuple(from_partner(w) for w in own_expert)

    state = block_state(series[0], qkv_own, norm_attn[None])
    pieces = exchange(state.reshape(seq_size, state.shape[0] // seq_size, HD), SEQ)
    before = prefix(pieces)
    states = exchange(before.reshape(seq_size * head_count, *before.shape[2:]), SEQ_HEAD)
    queries, inside = inside_block(series[0], norm_attn[None], qkv_own, qkv_other, own_rows)

    route_ids = expert_ids[0, :, 0]
    expert_count = router_weight.shape[1]
    capacity = 2 * own_rows // expert_count
    earlier_row = jnp.arange(own_rows)[None, :] < jnp.arange(own_rows)[:, None]
    same_expert = route_ids[:, None] == route_ids[None, :]
    slot_rank = jnp.sum(jnp.logical_and(same_expert, earlier_row), axis=1)
    slot_index = route_ids * capacity + slot_rank

    residual, normed_moe, send_buffer = mix_heads(
        queries,
        inside,
        states.reshape(before.shape),
        out_weight,
        out_other,
        series[0],
        norm_moe[None],
        slot_index[None, :],
        expert_count * capacity,
    )
    received = exchange(send_buffer.reshape(expert_count, capacity, width), SEQ_DP)

    logits = jnp.dot(normed_moe, router_weight, preferred_element_type=jnp.float32)
    picked_expert = route_ids[:, None] == jnp.arange(expert_count, dtype=jnp.int32)[None, :]
    gate_value = jax.nn.sigmoid(
        jnp.sum(jnp.where(picked_expert, logits, 0.0), axis=1, keepdims=True)
    )
    expert_out = expert_of(received.reshape(-1, width), own_expert, other_expert)
    returned = exchange(expert_out.reshape(received.shape), SEQ_DP)
    routing = (
        slot_index[:, None] == jnp.arange(expert_count * capacity, dtype=jnp.int32)[None, :]
    ).astype(jnp.bfloat16)
    routed = jnp.dot(
        routing,
        returned.reshape(expert_count * capacity, width),
        preferred_element_type=jnp.float32,
    )
    layer_out = (residual + gate_value * routed).astype(jnp.bfloat16)
    return layer_out[None]


def solution(mesh):
    split = Mesh(
        mesh.devices.reshape(8, 4, mesh.shape["head"], mesh.shape["dp"]),
        ("seq_0", "seq_1", "head", "dp"),
    )
    placed = (
        P("dp", SEQ, None),
        P(),
        P(None, None, "head"),
        P("head", None),
        P(),
        P(),
        P("dp", SEQ_HEAD, None),
        P(SEQ_DP, None, "head"),
        P(SEQ_DP, None, "head"),
        P(SEQ_DP, "head", None),
    )
    return jax.shard_map(
        on_device, mesh=split, in_specs=placed, out_specs=P("dp", SEQ_HEAD, None), check_vma=False
    )
```

```python
import math

import jax
import jax.numpy as jnp
from jax import lax
from jax.experimental import pallas as pl
from jax.experimental.pallas import tpu as pltpu
from jax.sharding import Mesh
from jax.sharding import PartitionSpec as P


HD = 128
SEQ = ("seq_0", "seq_1")
SEQ_DP = ("seq_0", "seq_1", "dp")
SEQ_HEAD = ("seq_0", "seq_1", "head")
NORM_EPS = 1e-06
FF_BLOCK = 512
MIB = 1024 * 1024


def from_partner(shard):
    return lax.ppermute(shard, "head", [(0, 1), (1, 0)])


def exchange(pieces, axes):
    return lax.all_to_all(pieces, axes, split_axis=0, concat_axis=0, tiled=True)


def expert_kernel(blocks, rows, gate_a, up_a, down_a, gate_b, up_b, down_b, out, total):
    step = pl.program_id(0)

    def add_part(gate, up, down):
        x = rows[...]
        g = jnp.dot(x, gate[...], preferred_element_type=jnp.float32)
        u = jnp.dot(x, up[...], preferred_element_type=jnp.float32)
        hidden = (g * (0.5 + 0.5 * jnp.tanh(0.5 * g)) * u).astype(jnp.bfloat16)
        return jnp.dot(hidden, down[...], preferred_element_type=jnp.float32)

    @pl.when(step == 0)
    def _():
        total[...] = add_part(gate_a, up_a, down_a)

    @pl.when(jnp.logical_and(step > 0, step < blocks))
    def _():
        total[...] += add_part(gate_a, up_a, down_a)

    @pl.when(step >= blocks)
    def _():
        total[...] += add_part(gate_b, up_b, down_b)

    @pl.when(step == 2 * blocks - 1)
    def _():
        out[...] = total[...].astype(out.dtype)


def expert_of(rows, own, partner):
    count, width = rows.shape
    units = own[0].shape[1]
    blocks = units // FF_BLOCK

    def first(step):
        return jnp.minimum(step, blocks - 1)

    def second(step):
        return jnp.maximum(step - blocks, 0)

    def specs(place):
        return [
            pl.BlockSpec((width, FF_BLOCK), lambda i: (0, place(i))),
            pl.BlockSpec((width, FF_BLOCK), lambda i: (0, place(i))),
            pl.BlockSpec((FF_BLOCK, width), lambda i: (place(i), 0)),
        ]

    return pl.pallas_call(
        lambda *refs: expert_kernel(blocks, *refs),
        grid=(2 * blocks,),
        in_specs=[pl.BlockSpec((count, width), lambda i: (0, 0))] + specs(first) + specs(second),
        out_specs=pl.BlockSpec((count, width), lambda i: (0, 0)),
        out_shape=jax.ShapeDtypeStruct((count, width), jnp.bfloat16),
        scratch_shapes=[pltpu.VMEM((count, width), jnp.float32)],
        compiler_params=pltpu.CompilerParams(
            dimension_semantics=("arbitrary",), vmem_limit_bytes=32 * MIB
        ),
        cost_estimate=pl.CostEstimate(
            flops=2 * count * width * units * 6,
            bytes_accessed=12 * width * units,
            transcendentals=2 * count * units,
        ),
        name="expert_mlp",
    )(rows, *(in_hbm(w) for w in own), *(in_hbm(w) for w in partner))


def in_hbm(array):
    return pltpu.with_memory_space_constraint(array, pltpu.HBM)


def normed_rows(rows, gain):
    x = rows.astype(jnp.float32)
    mean = jnp.sum(x * x, axis=-1, keepdims=True) * (1.0 / x.shape[1])
    return x * lax.rsqrt(mean + NORM_EPS) * gain.reshape(1, -1)


def state_kernel(series, weight, gain, state_out, rows, table, sems):
    half = table.shape[2]
    fetch_rows = pltpu.make_async_copy(series, rows, sems.at[0])
    fetch_keys = pltpu.make_async_copy(weight.at[1], table.at[0], sems.at[1])
    fetch_values = pltpu.make_async_copy(weight.at[2], table.at[1], sems.at[2])
    fetch_rows.start()
    fetch_keys.start()
    fetch_values.start()
    fetch_rows.wait()
    normed = normed_rows(rows[...], gain[...]).astype(jnp.bfloat16)
    fetch_keys.wait()
    keys = jnp.dot(normed, table[0], preferred_element_type=jnp.float32).astype(jnp.bfloat16)
    fetch_values.wait()
    values = jnp.dot(normed, table[1], preferred_element_type=jnp.float32).astype(jnp.bfloat16)
    heads = half // HD
    for n in range(heads):
        at = slice(n * HD, (n + 1) * HD)
        state_out[at, :] = lax.dot_general(
            keys[:, at], values[:, at], (((0,), (0,)), ((), ())), preferred_element_type=jnp.float32
        ).astype(jnp.bfloat16)
    state_out[heads * HD :, :] = jnp.zeros((HD, HD), jnp.bfloat16)


def block_state(series, weight, gain):
    count, width = series.shape
    half = weight.shape[2]
    return pl.pallas_call(
        state_kernel,
        in_specs=[
            pl.BlockSpec(memory_space=pl.ANY),
            pl.BlockSpec(memory_space=pl.ANY),
            pl.BlockSpec(memory_space=pltpu.VMEM),
        ],
        out_specs=pl.BlockSpec(memory_space=pltpu.VMEM),
        out_shape=jax.ShapeDtypeStruct((half + HD, HD), jnp.bfloat16),
        scratch_shapes=[
            pltpu.VMEM((count, width), jnp.bfloat16),
            pltpu.VMEM((2, width, half), jnp.bfloat16),
            pltpu.SemaphoreType.DMA((3,)),
        ],
        compiler_params=pltpu.CompilerParams(vmem_limit_bytes=24 * MIB),
        cost_estimate=pl.CostEstimate(
            flops=4 * count * width * half, bytes_accessed=4 * count * width, transcendentals=count
        ),
        name="block_state",
    )(in_hbm(series), in_hbm(weight), gain)


def prefix_kernel(pieces, out):
    total = jnp.zeros(pieces.shape[1:], jnp.float32)
    for k in range(pieces.shape[0]):
        rounded = total.astype(jnp.bfloat16)
        out[k] = rounded
        total = total + pieces[k].astype(jnp.float32)


def prefix(pieces):
    count, lines, lanes = pieces.shape
    return pl.pallas_call(
        prefix_kernel,
        in_specs=[pl.BlockSpec(memory_space=pltpu.VMEM)],
        out_specs=pl.BlockSpec(memory_space=pltpu.VMEM),
        out_shape=jax.ShapeDtypeStruct((count, lines, lanes), jnp.bfloat16),
        compiler_params=pltpu.CompilerParams(vmem_limit_bytes=4 * MIB),
        cost_estimate=pl.CostEstimate(
            flops=count * lines * lanes, bytes_accessed=6 * count * lines * lanes, transcendentals=0
        ),
        name="prefix",
    )(pieces)


def inside_kernel(
    series, gain, w_own, w_other, queries_out, inside_out, queries_held, inside_held, sems
):
    count, _ = series.shape
    own_rows = queries_held.shape[0]
    half = w_own.shape[2]
    heads = half // HD
    first_row = pl.multiple_of(lax.axis_index("head") * own_rows, own_rows)
    mine = normed_rows(series[pl.ds(first_row, own_rows), :], gain[...]).astype(jnp.bfloat16)
    normed = normed_rows(series[...], gain[...]).astype(jnp.bfloat16)
    row = lax.broadcasted_iota(jnp.int32, (own_rows, count), 0) + first_row
    causal = row >= lax.broadcasted_iota(jnp.int32, (own_rows, count), 1)
    for part, weight in ((0, w_own), (1, w_other)):
        queries, keys, values = (
            jnp.dot(rows, weight[k], preferred_element_type=jnp.float32).astype(jnp.bfloat16)
            for k, rows in ((0, mine), (1, normed), (2, normed))
        )
        queries_held[:, part * half : (part + 1) * half] = queries
        for n in range(heads):
            at = slice(n * HD, (n + 1) * HD)
            scores = lax.dot_general(
                queries[:, at],
                keys[:, at],
                (((1,), (1,)), ((), ())),
                preferred_element_type=jnp.float32,
            )
            scores = jnp.where(causal, scores, 0.0).astype(jnp.bfloat16)
            lanes = slice(part * half + n * HD, part * half + (n + 1) * HD)
            inside_held[:, lanes] = jnp.dot(
                scores, values[:, at], preferred_element_type=jnp.float32
            )
    keep_queries = pltpu.make_async_copy(queries_held, queries_out, sems.at[0])
    keep_inside = pltpu.make_async_copy(inside_held, inside_out, sems.at[1])
    keep_queries.start()
    keep_inside.start()
    keep_queries.wait()
    keep_inside.wait()


def inside_block(series, gain, w_own, w_other, own_rows):
    count, width = series.shape
    half = w_own.shape[2]
    return pl.pallas_call(
        inside_kernel,
        in_specs=[pl.BlockSpec(memory_space=pltpu.VMEM)] * 4,
        out_specs=[pl.BlockSpec(memory_space=pl.ANY)] * 2,
        out_shape=[
            pltpu.HBM((own_rows, 2 * half), jnp.bfloat16),
            pltpu.HBM((own_rows, 2 * half), jnp.float32),
        ],
        scratch_shapes=[
            pltpu.VMEM((own_rows, 2 * half), jnp.bfloat16),
            pltpu.VMEM((own_rows, 2 * half), jnp.float32),
            pltpu.SemaphoreType.DMA((2,)),
        ],
        compiler_params=pltpu.CompilerParams(vmem_limit_bytes=24 * MIB),
        cost_estimate=pl.CostEstimate(
            flops=10 * count * width * half + 8 * own_rows * count * half,
            bytes_accessed=8 * count * width,
            transcendentals=0,
        ),
        name="inside_block",
    )(series, gain, w_own, w_other)


def mix_kernel(
    queries,
    inside,
    state_own,
    state_other,
    out_own,
    out_other,
    series,
    gain,
    slots,
    residual_out,
    normed_out,
    send_out,
    queries_in,
    inside_in,
    residual_held,
    normed_held,
    sems,
):
    own_rows, _ = queries_in.shape
    half = out_own.shape[0]
    heads = half // HD
    first_row = pl.multiple_of(lax.axis_index("head") * own_rows, own_rows)
    fetches = [
        pltpu.make_async_copy(queries, queries_in, sems.at[0]),
        pltpu.make_async_copy(inside, inside_in, sems.at[1]),
    ]
    for fetch in fetches:
        fetch.start()
    base = lax.axis_index(SEQ) * series.shape[0] + first_row + 1
    position = lax.broadcasted_iota(jnp.int32, (own_rows, HD), 0) + base
    unit = 1.0 / (position.astype(jnp.float32) * math.sqrt(HD))
    slot = lax.broadcasted_iota(jnp.int32, (send_out.shape[0], own_rows), 0)
    chosen = jnp.where(slot == slots[...], 1.0, 0.0).astype(jnp.bfloat16)
    fetches[0].wait()
    fetches[1].wait()
    mixed = []
    for part, state in ((0, state_own), (1, state_other)):
        for n in range(heads):
            lanes = slice(part * half + n * HD, part * half + (n + 1) * HD)
            start = state[n * HD : (n + 1) * HD, :]
            carried = jnp.dot(queries_in[:, lanes], start, preferred_element_type=jnp.float32)
            mixed.append(((inside_in[:, lanes] + carried) * unit).astype(jnp.bfloat16))
    total = series[pl.ds(first_row, own_rows), :].astype(jnp.float32)
    for mine, weight in ((mixed[:heads], out_own), (mixed[heads:], out_other)):
        total += jnp.dot(
            jnp.concatenate(mine, axis=1), weight[...], preferred_element_type=jnp.float32
        )
    residual_held[...] = total
    keep_residual = pltpu.make_async_copy(residual_held, residual_out, sems.at[2])
    keep_residual.start()
    normed = normed_rows(total, gain[...]).astype(jnp.bfloat16)
    normed_held[...] = normed
    keep_normed = pltpu.make_async_copy(normed_held, normed_out, sems.at[3])
    keep_normed.start()
    send_out[...] = jnp.dot(chosen, normed, preferred_element_type=jnp.float32).astype(
        jnp.bfloat16
    )
    keep_residual.wait()
    keep_normed.wait()


def mix_heads(
    queries, inside, state_own, state_other, out_own, out_other, series, gain, slots, slot_count
):
    own_rows, width = queries.shape
    anywhere = pl.BlockSpec(memory_space=pl.ANY)
    local = pl.BlockSpec(memory_space=pltpu.VMEM)
    return pl.pallas_call(
        mix_kernel,
        in_specs=[anywhere] * 2 + [local] * 7,
        out_specs=[anywhere, anywhere, local],
        out_shape=[
            pltpu.HBM((own_rows, width), jnp.float32),
            pltpu.HBM((own_rows, width), jnp.bfloat16),
            jax.ShapeDtypeStruct((slot_count, width), jnp.bfloat16),
        ],
        scratch_shapes=[
            pltpu.VMEM((own_rows, width), jnp.bfloat16),
            pltpu.VMEM((own_rows, width), jnp.float32),
            pltpu.VMEM((own_rows, width), jnp.float32),
            pltpu.VMEM((own_rows, width), jnp.bfloat16),
            pltpu.SemaphoreType.DMA((4,)),
        ],
        compiler_params=pltpu.CompilerParams(vmem_limit_bytes=24 * MIB),
        cost_estimate=pl.CostEstimate(
            flops=2 * own_rows * width * (width + HD + slot_count),
            bytes_accessed=12 * own_rows * width,
            transcendentals=own_rows,
        ),
        name="mix_heads",
    )(
        in_hbm(queries),
        in_hbm(inside),
        state_own,
        state_other,
        out_own,
        out_other,
        series,
        gain,
        slots,
    )


def on_device(
    series,
    norm_attn,
    qkv_weight,
    out_weight,
    norm_moe,
    router_weight,
    expert_ids,
    gate_weight,
    up_weight,
    down_weight,
):
    width = series.shape[2]
    head_count = lax.axis_size("head")
    seq_size = lax.axis_size(SEQ)
    own_rows = series.shape[1] // head_count

    qkv_own = jnp.moveaxis(qkv_weight, 1, 0)
    qkv_other = from_partner(qkv_own)
    out_other = from_partner(out_weight)
    own_expert = (gate_weight[0], up_weight[0], down_weight[0])
    other_expert = tuple(from_partner(w) for w in own_expert)

    state = block_state(series[0], qkv_own, norm_attn)
    pieces = exchange(state.reshape(seq_size, state.shape[0] // seq_size, HD), SEQ)
    state_own = exchange(prefix(pieces), SEQ)
    state_other = from_partner(state_own)
    queries, inside = inside_block(series[0], norm_attn, qkv_own, qkv_other, own_rows)

    route_ids = expert_ids[0, :, 0]
    expert_count = router_weight.shape[1]
    capacity = 2 * own_rows // expert_count
    earlier_row = jnp.arange(own_rows)[None, :] < jnp.arange(own_rows)[:, None]
    same_expert = route_ids[:, None] == route_ids[None, :]
    slot_rank = jnp.sum(jnp.logical_and(same_expert, earlier_row), axis=1)
    slot_index = route_ids * capacity + slot_rank

    residual, normed_moe, send_buffer = mix_heads(
        queries,
        inside,
        state_own.reshape(state.shape),
        state_other.reshape(state.shape),
        out_weight,
        out_other,
        series[0],
        norm_moe,
        slot_index[None, :],
        expert_count * capacity,
    )
    received = exchange(send_buffer.reshape(expert_count, capacity, width), SEQ_DP)

    logits = jnp.dot(normed_moe, router_weight, preferred_element_type=jnp.float32)
    picked_expert = route_ids[:, None] == jnp.arange(expert_count, dtype=jnp.int32)[None, :]
    gate_value = jax.nn.sigmoid(
        jnp.sum(jnp.where(picked_expert, logits, 0.0), axis=1, keepdims=True)
    )
    expert_out = expert_of(received.reshape(-1, width), own_expert, other_expert)
    returned = exchange(expert_out.reshape(received.shape), SEQ_DP)
    routing = (
        slot_index[:, None] == jnp.arange(expert_count * capacity, dtype=jnp.int32)[None, :]
    ).astype(jnp.bfloat16)
    routed = jnp.dot(
        routing,
        returned.reshape(expert_count * capacity, width),
        preferred_element_type=jnp.float32,
    )
    layer_out = (residual + gate_value * routed).astype(jnp.bfloat16)
    return layer_out[None]


def solution(mesh):
    split = Mesh(
        mesh.devices.reshape(8, 4, mesh.shape["head"], mesh.shape["dp"]),
        ("seq_0", "seq_1", "head", "dp"),
    )
    placed = (
        P("dp", SEQ, None),
        P(),
        P(None, None, "head"),
        P("head", None),
        P(),
        P(),
        P("dp", SEQ_HEAD, None),
        P(SEQ_DP, None, "head"),
        P(SEQ_DP, None, "head"),
        P(SEQ_DP, "head", None),
    )

    return jax.shard_map(
        on_device, mesh=split, in_specs=placed, out_specs=P("dp", SEQ_HEAD, None), check_vma=False
    )
```

```python
import math

import jax
import jax.numpy as jnp
from jax import lax
from jax.experimental import pallas as pl
from jax.experimental.pallas import tpu as pltpu
from jax.sharding import Mesh
from jax.sharding import PartitionSpec as P


HD = 128
SEQ = ("seq_0", "seq_1")
SEQ_DP = ("seq_0", "seq_1", "dp")
SEQ_HEAD = ("seq_0", "seq_1", "head")
NORM_EPS = 1e-06
FF_BLOCK = 512
MIB = 1024 * 1024


def from_partner(shard):
    return lax.ppermute(shard, "head", [(0, 1), (1, 0)])


def exchange(pieces, axes):
    return lax.all_to_all(pieces, axes, split_axis=0, concat_axis=0, tiled=True)


def expert_kernel(rows, gate_a, up_a, down_a, gate_b, up_b, down_b, out, gate, up, down, total, sems):
    blocks = gate.shape[0]
    own_blocks = blocks // 2
    first = FF_BLOCK // 2

    def copies(k):
        gates, ups, downs = (gate_a, up_a, down_a) if k < own_blocks else (gate_b, up_b, down_b)
        base = (k % own_blocks) * FF_BLOCK
        spans = ((0, first), (first, first)) if k == 0 else ((0, FF_BLOCK),)
        for n, (at, size) in enumerate(spans):
            row = 0 if k == 0 and n == 0 else k + 1
            to, source = pl.ds(at, size), pl.ds(base + at, size)
            yield pltpu.make_async_copy(gates.at[:, source], gate.at[k, :, to], sems.at[row, 0])
            yield pltpu.make_async_copy(ups.at[:, source], up.at[k, :, to], sems.at[row, 1])
            yield pltpu.make_async_copy(downs.at[source, :], down.at[k, to, :], sems.at[row, 2])

    started = [list(copies(k)) for k in range(blocks)]
    for some in started:
        for copy in some:
            copy.start()

    def part(gates, ups, downs):
        x = rows[...]
        g = jnp.dot(x, gates, preferred_element_type=jnp.float32)
        u = jnp.dot(x, ups, preferred_element_type=jnp.float32)
        hidden = (g * (0.5 + 0.5 * jnp.tanh(0.5 * g)) * u).astype(jnp.bfloat16)
        return jnp.dot(hidden, downs, preferred_element_type=jnp.float32)

    for copy in started[0][:3]:
        copy.wait()
    total[...] = part(gate[0, :, :first], up[0, :, :first], down[0, :first, :])
    for copy in started[0][3:]:
        copy.wait()
    total[...] += part(gate[0, :, first:], up[0, :, first:], down[0, first:, :])

    def step(k, carry):
        whole = pl.ds(0, FF_BLOCK)
        pltpu.make_async_copy(gate_a.at[:, whole], gate.at[k], sems.at[k + 1, 0]).wait()
        pltpu.make_async_copy(up_a.at[:, whole], up.at[k], sems.at[k + 1, 1]).wait()
        pltpu.make_async_copy(down_a.at[whole, :], down.at[k], sems.at[k + 1, 2]).wait()
        total[...] += part(gate[k], up[k], down[k])
        return carry

    lax.fori_loop(1, blocks, step, 0)
    out[...] = total[...].astype(out.dtype)


def expert_of(rows, own, partner):
    count, width = rows.shape
    units = own[0].shape[1]
    blocks = 2 * units // FF_BLOCK
    local = pl.BlockSpec(memory_space=pltpu.VMEM)
    return pl.pallas_call(
        expert_kernel,
        in_specs=[local] + [pl.BlockSpec(memory_space=pl.ANY)] * 6,
        out_specs=local,
        out_shape=jax.ShapeDtypeStruct((count, width), jnp.bfloat16),
        scratch_shapes=[
            pltpu.VMEM((blocks, width, FF_BLOCK), jnp.bfloat16),
            pltpu.VMEM((blocks, width, FF_BLOCK), jnp.bfloat16),
            pltpu.VMEM((blocks, FF_BLOCK, width), jnp.bfloat16),
            pltpu.VMEM((count, width), jnp.float32),
            pltpu.SemaphoreType.DMA((blocks + 1, 3)),
        ],
        compiler_params=pltpu.CompilerParams(vmem_limit_bytes=36 * MIB),
        cost_estimate=pl.CostEstimate(
            flops=2 * count * width * units * 6,
            bytes_accessed=12 * width * units,
            transcendentals=2 * count * units,
        ),
        name="expert_mlp",
    )(rows, *(in_hbm(w) for w in own), *(in_hbm(w) for w in partner))


def in_parts(source, target, sems, parts):
    size = source.shape[0] // parts
    return [
        pltpu.make_async_copy(
            source.at[pl.ds(k * size, size)], target.at[pl.ds(k * size, size)], sems.at[k]
        )
        for k in range(parts)
    ]


def in_hbm(array):
    return pltpu.with_memory_space_constraint(array, pltpu.HBM)


def normed_rows(rows, gain):
    x = rows.astype(jnp.float32)
    mean = jnp.sum(x * x, axis=-1, keepdims=True) * (1.0 / x.shape[1])
    return x * lax.rsqrt(mean + NORM_EPS) * gain.reshape(1, -1)


def state_kernel(series, weight, gain, state_out, rows, table, sems):
    half = table.shape[2]
    fetches = [
        in_parts(series, rows, sems.at[0], 4),
        in_parts(weight.at[1], table.at[0], sems.at[1], 4),
        in_parts(weight.at[2], table.at[1], sems.at[2], 4),
    ]
    for some in fetches:
        for fetch in some:
            fetch.start()
    for fetch in fetches[0]:
        fetch.wait()
    normed = normed_rows(rows[...], gain[...]).astype(jnp.bfloat16)
    for fetch in fetches[1]:
        fetch.wait()
    keys = jnp.dot(normed, table[0], preferred_element_type=jnp.float32).astype(jnp.bfloat16)
    for fetch in fetches[2]:
        fetch.wait()
    values = jnp.dot(normed, table[1], preferred_element_type=jnp.float32).astype(jnp.bfloat16)
    heads = half // HD
    for n in range(heads):
        at = slice(n * HD, (n + 1) * HD)
        state_out[at, :] = lax.dot_general(
            keys[:, at], values[:, at], (((0,), (0,)), ((), ())), preferred_element_type=jnp.float32
        ).astype(jnp.bfloat16)
    state_out[heads * HD :, :] = jnp.zeros((HD, HD), jnp.bfloat16)


def block_state(series, weight, gain):
    count, width = series.shape
    half = weight.shape[2]
    return pl.pallas_call(
        state_kernel,
        in_specs=[
            pl.BlockSpec(memory_space=pl.ANY),
            pl.BlockSpec(memory_space=pl.ANY),
            pl.BlockSpec(memory_space=pltpu.VMEM),
        ],
        out_specs=pl.BlockSpec(memory_space=pltpu.VMEM),
        out_shape=jax.ShapeDtypeStruct((half + HD, HD), jnp.bfloat16),
        scratch_shapes=[
            pltpu.VMEM((count, width), jnp.bfloat16),
            pltpu.VMEM((2, width, half), jnp.bfloat16),
            pltpu.SemaphoreType.DMA((3, 4)),
        ],
        compiler_params=pltpu.CompilerParams(vmem_limit_bytes=24 * MIB),
        cost_estimate=pl.CostEstimate(
            flops=4 * count * width * half, bytes_accessed=4 * count * width, transcendentals=count
        ),
        name="block_state",
    )(in_hbm(series), in_hbm(weight), gain)


def prefix_kernel(pieces, out):
    total = jnp.zeros(pieces.shape[1:], jnp.float32)
    for k in range(pieces.shape[0]):
        rounded = total.astype(jnp.bfloat16)
        out[k] = rounded
        total = total + pieces[k].astype(jnp.float32)


def prefix(pieces):
    count, lines, lanes = pieces.shape
    return pl.pallas_call(
        prefix_kernel,
        in_specs=[pl.BlockSpec(memory_space=pltpu.VMEM)],
        out_specs=pl.BlockSpec(memory_space=pltpu.VMEM),
        out_shape=jax.ShapeDtypeStruct((count, lines, lanes), jnp.bfloat16),
        compiler_params=pltpu.CompilerParams(vmem_limit_bytes=4 * MIB),
        cost_estimate=pl.CostEstimate(
            flops=count * lines * lanes, bytes_accessed=6 * count * lines * lanes, transcendentals=0
        ),
        name="prefix",
    )(pieces)


def inside_kernel(
    series, gain, w_own, w_other, queries_out, inside_out, queries_held, inside_held, sems
):
    count, _ = series.shape
    own_rows = queries_held.shape[0]
    half = w_own.shape[2]
    heads = half // HD
    first_row = pl.multiple_of(lax.axis_index("head") * own_rows, own_rows)
    mine = normed_rows(series[pl.ds(first_row, own_rows), :], gain[...]).astype(jnp.bfloat16)
    normed = normed_rows(series[...], gain[...]).astype(jnp.bfloat16)
    row = lax.broadcasted_iota(jnp.int32, (own_rows, count), 0) + first_row
    causal = row >= lax.broadcasted_iota(jnp.int32, (own_rows, count), 1)
    for part, weight in ((0, w_own), (1, w_other)):
        queries, keys, values = (
            jnp.dot(rows, weight[k], preferred_element_type=jnp.float32).astype(jnp.bfloat16)
            for k, rows in ((0, mine), (1, normed), (2, normed))
        )
        queries_held[:, part * half : (part + 1) * half] = queries
        for n in range(heads):
            at = slice(n * HD, (n + 1) * HD)
            scores = lax.dot_general(
                queries[:, at],
                keys[:, at],
                (((1,), (1,)), ((), ())),
                preferred_element_type=jnp.float32,
            )
            scores = jnp.where(causal, scores, 0.0).astype(jnp.bfloat16)
            lanes = slice(part * half + n * HD, part * half + (n + 1) * HD)
            inside_held[:, lanes] = jnp.dot(
                scores, values[:, at], preferred_element_type=jnp.float32
            )
    keep_queries = pltpu.make_async_copy(queries_held, queries_out, sems.at[0])
    keep_inside = pltpu.make_async_copy(inside_held, inside_out, sems.at[1])
    keep_queries.start()
    keep_inside.start()
    keep_queries.wait()
    keep_inside.wait()


def inside_block(series, gain, w_own, w_other, own_rows):
    count, width = series.shape
    half = w_own.shape[2]
    return pl.pallas_call(
        inside_kernel,
        in_specs=[pl.BlockSpec(memory_space=pltpu.VMEM)] * 4,
        out_specs=[pl.BlockSpec(memory_space=pl.ANY)] * 2,
        out_shape=[
            pltpu.HBM((own_rows, 2 * half), jnp.bfloat16),
            pltpu.HBM((own_rows, 2 * half), jnp.float32),
        ],
        scratch_shapes=[
            pltpu.VMEM((own_rows, 2 * half), jnp.bfloat16),
            pltpu.VMEM((own_rows, 2 * half), jnp.float32),
            pltpu.SemaphoreType.DMA((2,)),
        ],
        compiler_params=pltpu.CompilerParams(vmem_limit_bytes=24 * MIB),
        cost_estimate=pl.CostEstimate(
            flops=10 * count * width * half + 8 * own_rows * count * half,
            bytes_accessed=8 * count * width,
            transcendentals=0,
        ),
        name="inside_block",
    )(series, gain, w_own, w_other)


def mix_kernel(
    queries,
    inside,
    state_own,
    state_other,
    out_own,
    out_other,
    series,
    gain,
    slots,
    ids,
    router,
    residual_out,
    gate_out,
    send_out,
    queries_in,
    inside_in,
    weights_in,
    rows_in,
    residual_held,
    gate_held,
    sems,
):
    own_rows, _ = rows_in.shape
    half = out_own.shape[0]
    heads = half // HD
    first_row = pl.multiple_of(lax.axis_index("head") * own_rows, own_rows)
    fetches = [
        in_parts(queries, queries_in, sems.at[0], 2),
        in_parts(inside, inside_in, sems.at[1], 4),
        in_parts(out_own, weights_in.at[0], sems.at[2], 2),
        in_parts(out_other, weights_in.at[1], sems.at[3], 2),
        in_parts(series.at[pl.ds(first_row, own_rows)], rows_in, sems.at[4], 2),
    ]
    for some in fetches:
        for fetch in some:
            fetch.start()

    def arrived(k):
        for fetch in fetches[k]:
            fetch.wait()

    base = lax.axis_index(SEQ) * series.shape[0] + first_row + 1
    position = lax.broadcasted_iota(jnp.int32, (own_rows, HD), 0) + base
    unit = 1.0 / (position.astype(jnp.float32) * math.sqrt(HD))
    slot = lax.broadcasted_iota(jnp.int32, (send_out.shape[0], own_rows), 0)
    chosen = jnp.where(slot == slots[...], 1.0, 0.0).astype(jnp.bfloat16)
    arrived(0)
    carried = []
    for part, state in ((0, state_own), (1, state_other)):
        for n in range(heads):
            lanes = slice(part * half + n * HD, part * half + (n + 1) * HD)
            start = state[n * HD : (n + 1) * HD, :]
            carried.append(
                jnp.dot(queries_in[:, lanes], start, preferred_element_type=jnp.float32)
            )
    arrived(1)
    mixed = [
        ((inside_in[:, k * HD : (k + 1) * HD] + carried[k]) * unit).astype(jnp.bfloat16)
        for k in range(2 * heads)
    ]
    arrived(2)
    total = jnp.dot(
        jnp.concatenate(mixed[:heads], axis=1), weights_in[0], preferred_element_type=jnp.float32
    )
    arrived(3)
    total += jnp.dot(
        jnp.concatenate(mixed[heads:], axis=1), weights_in[1], preferred_element_type=jnp.float32
    )
    arrived(4)
    total += rows_in[...].astype(jnp.float32)
    residual_held[...] = total
    keep_residual = in_parts(residual_held, residual_out, sems.at[5], 4)
    for keep in keep_residual:
        keep.start()
    normed = normed_rows(total, gain[...]).astype(jnp.bfloat16)
    logits = jnp.dot(normed, router[...], preferred_element_type=jnp.float32)
    expert = lax.broadcasted_iota(jnp.int32, logits.shape, 1)
    logit = jnp.sum(jnp.where(expert == ids[...], logits, 0.0), axis=1, keepdims=True)
    gate_held[...] = jnp.broadcast_to(jax.nn.sigmoid(logit), gate_held.shape)
    keep_gate = pltpu.make_async_copy(gate_held, gate_out, sems.at[6, 0])
    keep_gate.start()
    send_out[...] = jnp.dot(chosen, normed, preferred_element_type=jnp.float32).astype(
        jnp.bfloat16
    )
    for keep in keep_residual:
        keep.wait()
    keep_gate.wait()


def mix_heads(
    queries,
    inside,
    state_own,
    state_other,
    out_own,
    out_other,
    series,
    gain,
    slots,
    ids,
    router,
    slot_count,
):
    own_rows, width = queries.shape
    half = out_own.shape[0]
    anywhere = pl.BlockSpec(memory_space=pl.ANY)
    local = pl.BlockSpec(memory_space=pltpu.VMEM)
    return pl.pallas_call(
        mix_kernel,
        in_specs=[anywhere] * 2 + [local] * 2 + [anywhere] * 3 + [local] * 4,
        out_specs=[anywhere, anywhere, local],
        out_shape=[
            pltpu.HBM((own_rows, width), jnp.float32),
            pltpu.HBM((own_rows, HD), jnp.float32),
            jax.ShapeDtypeStruct((slot_count, width), jnp.bfloat16),
        ],
        scratch_shapes=[
            pltpu.VMEM((own_rows, width), jnp.bfloat16),
            pltpu.VMEM((own_rows, width), jnp.float32),
            pltpu.VMEM((2, half, width), jnp.bfloat16),
            pltpu.VMEM((own_rows, width), jnp.bfloat16),
            pltpu.VMEM((own_rows, width), jnp.float32),
            pltpu.VMEM((own_rows, HD), jnp.float32),
            pltpu.SemaphoreType.DMA((7, 4)),
        ],
        compiler_params=pltpu.CompilerParams(vmem_limit_bytes=24 * MIB),
        cost_estimate=pl.CostEstimate(
            flops=2 * own_rows * width * (width + 2 * HD + slot_count),
            bytes_accessed=12 * own_rows * width,
            transcendentals=own_rows,
        ),
        name="mix_heads",
    )(
        in_hbm(queries),
        in_hbm(inside),
        state_own,
        state_other,
        in_hbm(out_own),
        in_hbm(out_other),
        in_hbm(series),
        gain,
        slots,
        ids,
        router,
    )


def combine_kernel(returned, residual, gate, slots, out, residual_in, gate_in, held, sems):
    own_rows, width = residual_in.shape
    fetches = in_parts(residual, residual_in, sems.at[0], 4)
    fetch_gate = pltpu.make_async_copy(gate, gate_in, sems.at[1, 0])
    for fetch in fetches:
        fetch.start()
    fetch_gate.start()
    slot = lax.broadcasted_iota(jnp.int32, (returned.shape[0], own_rows), 0)
    chosen = jnp.where(slot == slots[...], 1.0, 0.0).astype(jnp.bfloat16)
    routed = lax.dot_general(
        chosen, returned[...], (((0,), (0,)), ((), ())), preferred_element_type=jnp.float32
    )
    fetch_gate.wait()
    for fetch in fetches:
        fetch.wait()
    weight = jnp.concatenate([gate_in[...]] * (width // HD), axis=1)
    held[...] = (residual_in[...] + weight * routed).astype(jnp.bfloat16)
    leave = in_parts(held, out, sems.at[2], 4)
    for copy in leave:
        copy.start()
    for copy in leave:
        copy.wait()


def combine(returned, residual, gate, slots):
    own_rows, width = residual.shape
    anywhere = pl.BlockSpec(memory_space=pl.ANY)
    local = pl.BlockSpec(memory_space=pltpu.VMEM)
    return pl.pallas_call(
        combine_kernel,
        in_specs=[local, anywhere, anywhere, local],
        out_specs=anywhere,
        out_shape=pltpu.HBM((own_rows, width), jnp.bfloat16),
        scratch_shapes=[
            pltpu.VMEM((own_rows, width), jnp.float32),
            pltpu.VMEM((own_rows, HD), jnp.float32),
            pltpu.VMEM((own_rows, width), jnp.bfloat16),
            pltpu.SemaphoreType.DMA((3, 4)),
        ],
        compiler_params=pltpu.CompilerParams(vmem_limit_bytes=24 * MIB),
        cost_estimate=pl.CostEstimate(
            flops=2 * own_rows * width * returned.shape[0],
            bytes_accessed=10 * own_rows * width,
            transcendentals=0,
        ),
        name="combine",
    )(returned, in_hbm(residual), in_hbm(gate), slots)


def on_device(
    series,
    norm_attn,
    qkv_weight,
    out_weight,
    norm_moe,
    router_weight,
    expert_ids,
    gate_weight,
    up_weight,
    down_weight,
):
    width = series.shape[2]
    head_count = lax.axis_size("head")
    seq_size = lax.axis_size(SEQ)
    own_rows = series.shape[1] // head_count

    qkv_own = jnp.moveaxis(qkv_weight, 1, 0)
    qkv_other = from_partner(qkv_own)
    out_other = from_partner(out_weight)
    own_expert = (gate_weight[0], up_weight[0], down_weight[0])
    other_expert = tuple(from_partner(w) for w in own_expert)

    state = block_state(series[0], qkv_own, norm_attn)
    pieces = exchange(state.reshape(seq_size, state.shape[0] // seq_size, HD), SEQ)
    state_own = exchange(prefix(pieces), SEQ)
    state_other = from_partner(state_own)
    queries, inside = inside_block(series[0], norm_attn, qkv_own, qkv_other, own_rows)

    route_ids = expert_ids[0, :, 0]
    expert_count = router_weight.shape[1]
    capacity = 2 * own_rows // expert_count
    earlier_row = jnp.arange(own_rows)[None, :] < jnp.arange(own_rows)[:, None]
    same_expert = route_ids[:, None] == route_ids[None, :]
    slot_rank = jnp.sum(jnp.logical_and(same_expert, earlier_row), axis=1)
    slot_index = route_ids * capacity + slot_rank

    slots = slot_index[None, :]
    residual, gate, send_buffer = mix_heads(
        queries,
        inside,
        state_own.reshape(state.shape),
        state_other.reshape(state.shape),
        out_weight,
        out_other,
        series[0],
        norm_moe,
        slots,
        route_ids[:, None],
        router_weight,
        expert_count * capacity,
    )
    received = exchange(send_buffer.reshape(expert_count, capacity, width), SEQ_DP)

    expert_out = expert_of(received.reshape(-1, width), own_expert, other_expert)
    returned = exchange(expert_out.reshape(received.shape), SEQ_DP)
    layer_out = combine(returned.reshape(send_buffer.shape), residual, gate, slots)
    return layer_out[None]


def solution(mesh):
    split = Mesh(
        mesh.devices.reshape(8, 4, mesh.shape["head"], mesh.shape["dp"]),
        ("seq_0", "seq_1", "head", "dp"),
    )
    placed = (
        P("dp", SEQ, None),
        P(),
        P(None, None, "head"),
        P("head", None),
        P(),
        P(),
        P("dp", SEQ_HEAD, None),
        P(SEQ_DP, None, "head"),
        P(SEQ_DP, None, "head"),
        P(SEQ_DP, "head", None),
    )

    return jax.shard_map(
        on_device, mesh=split, in_specs=placed, out_specs=P("dp", SEQ_HEAD, None), check_vma=False
    )
```

```python
import math

import jax
import jax.numpy as jnp
from jax import lax
from jax.experimental import pallas as pl
from jax.experimental.pallas import tpu as pltpu
from jax.sharding import Mesh
from jax.sharding import PartitionSpec as P


HD = 128
SEQ = ("seq_0", "seq_1")
SEQ_DP = ("seq_0", "seq_1", "dp")
SEQ_HEAD = ("seq_0", "seq_1", "head")
NORM_EPS = 1e-06
FF_BLOCK = 512
MIB = 1024 * 1024


def from_partner(shard):
    return lax.ppermute(shard, "head", [(0, 1), (1, 0)])


def exchange(pieces, axes):
    return lax.all_to_all(pieces, axes, split_axis=0, concat_axis=0, tiled=True)


def expert_kernel(rows, gate_a, up_a, down_a, gate_b, up_b, down_b, out, gate, up, down, total, sems):
    blocks = gate.shape[0]
    own_blocks = blocks // 2
    first = FF_BLOCK // 2

    def copies(k):
        gates, ups, downs = (gate_a, up_a, down_a) if k < own_blocks else (gate_b, up_b, down_b)
        base = (k % own_blocks) * FF_BLOCK
        spans = ((0, first), (first, first)) if k == 0 else ((0, FF_BLOCK),)
        for n, (at, size) in enumerate(spans):
            row = 0 if k == 0 and n == 0 else k + 1
            to, source = pl.ds(at, size), pl.ds(base + at, size)
            yield pltpu.make_async_copy(gates.at[:, source], gate.at[k, :, to], sems.at[row, 0])
            yield pltpu.make_async_copy(ups.at[:, source], up.at[k, :, to], sems.at[row, 1])
            yield pltpu.make_async_copy(downs.at[source, :], down.at[k, to, :], sems.at[row, 2])

    started = [list(copies(k)) for k in range(blocks)]
    for some in started:
        for copy in some:
            copy.start()

    def part(gates, ups, downs):
        x = rows[...]
        g = jnp.dot(x, gates, preferred_element_type=jnp.float32)
        u = jnp.dot(x, ups, preferred_element_type=jnp.float32)
        hidden = (g * (0.5 + 0.5 * jnp.tanh(0.5 * g)) * u).astype(jnp.bfloat16)
        return jnp.dot(hidden, downs, preferred_element_type=jnp.float32)

    for copy in started[0][:3]:
        copy.wait()
    total[...] = part(gate[0, :, :first], up[0, :, :first], down[0, :first, :])
    for copy in started[0][3:]:
        copy.wait()
    total[...] += part(gate[0, :, first:], up[0, :, first:], down[0, first:, :])

    def step(k, carry):
        whole = pl.ds(0, FF_BLOCK)
        pltpu.make_async_copy(gate_a.at[:, whole], gate.at[k], sems.at[k + 1, 0]).wait()
        pltpu.make_async_copy(up_a.at[:, whole], up.at[k], sems.at[k + 1, 1]).wait()
        pltpu.make_async_copy(down_a.at[whole, :], down.at[k], sems.at[k + 1, 2]).wait()
        total[...] += part(gate[k], up[k], down[k])
        return carry

    lax.fori_loop(1, blocks, step, 0)
    out[...] = total[...].astype(out.dtype)


def expert_of(rows, own, partner):
    count, width = rows.shape
    units = own[0].shape[1]
    blocks = 2 * units // FF_BLOCK
    local = pl.BlockSpec(memory_space=pltpu.VMEM)
    return pl.pallas_call(
        expert_kernel,
        in_specs=[local] + [pl.BlockSpec(memory_space=pl.ANY)] * 6,
        out_specs=local,
        out_shape=jax.ShapeDtypeStruct((count, width), jnp.bfloat16),
        scratch_shapes=[
            pltpu.VMEM((blocks, width, FF_BLOCK), jnp.bfloat16),
            pltpu.VMEM((blocks, width, FF_BLOCK), jnp.bfloat16),
            pltpu.VMEM((blocks, FF_BLOCK, width), jnp.bfloat16),
            pltpu.VMEM((count, width), jnp.float32),
            pltpu.SemaphoreType.DMA((blocks + 1, 3)),
        ],
        compiler_params=pltpu.CompilerParams(vmem_limit_bytes=36 * MIB),
        cost_estimate=pl.CostEstimate(
            flops=2 * count * width * units * 6,
            bytes_accessed=12 * width * units,
            transcendentals=2 * count * units,
        ),
        name="expert_mlp",
    )(rows, *(in_hbm(w) for w in own), *(in_hbm(w) for w in partner))


def in_parts(source, target, sems, parts):
    size = source.shape[0] // parts
    return [
        pltpu.make_async_copy(
            source.at[pl.ds(k * size, size)], target.at[pl.ds(k * size, size)], sems.at[k]
        )
        for k in range(parts)
    ]


def in_hbm(array):
    return pltpu.with_memory_space_constraint(array, pltpu.HBM)


def normed_rows(rows, gain):
    x = rows.astype(jnp.float32)
    mean = jnp.sum(x * x, axis=-1, keepdims=True) * (1.0 / x.shape[1])
    return x * lax.rsqrt(mean + NORM_EPS) * gain.reshape(1, -1)


def state_kernel(series, weight, gain, state_out, rows, table, gain_in, sems):
    half = table.shape[2]
    fetches = [
        in_parts(series, rows, sems.at[0], 4),
        in_parts(weight.at[1], table.at[0], sems.at[1], 4),
        in_parts(weight.at[2], table.at[1], sems.at[2], 4),
    ]
    fetch_gain = pltpu.make_async_copy(gain, gain_in, sems.at[3, 0])
    for fetch in fetches[0]:
        fetch.start()
    fetch_gain.start()
    for some in fetches[1:]:
        for fetch in some:
            fetch.start()
    for fetch in fetches[0]:
        fetch.wait()
    fetch_gain.wait()
    normed = normed_rows(rows[...], gain_in[...]).astype(jnp.bfloat16)
    for fetch in fetches[1]:
        fetch.wait()
    keys = jnp.dot(normed, table[0], preferred_element_type=jnp.float32).astype(jnp.bfloat16)
    for fetch in fetches[2]:
        fetch.wait()
    values = jnp.dot(normed, table[1], preferred_element_type=jnp.float32).astype(jnp.bfloat16)
    heads = half // HD
    for n in range(heads):
        at = slice(n * HD, (n + 1) * HD)
        state_out[at, :] = lax.dot_general(
            keys[:, at], values[:, at], (((0,), (0,)), ((), ())), preferred_element_type=jnp.float32
        ).astype(jnp.bfloat16)
    state_out[heads * HD :, :] = jnp.zeros((HD, HD), jnp.bfloat16)


def block_state(series, weight, gain):
    count, width = series.shape
    half = weight.shape[2]
    return pl.pallas_call(
        state_kernel,
        in_specs=[
            pl.BlockSpec(memory_space=pl.ANY),
            pl.BlockSpec(memory_space=pl.ANY),
            pl.BlockSpec(memory_space=pl.ANY),
        ],
        out_specs=pl.BlockSpec(memory_space=pltpu.VMEM),
        out_shape=jax.ShapeDtypeStruct((half + HD, HD), jnp.bfloat16),
        scratch_shapes=[
            pltpu.VMEM((count, width), jnp.bfloat16),
            pltpu.VMEM((2, width, half), jnp.bfloat16),
            pltpu.VMEM((width,), jnp.float32),
            pltpu.SemaphoreType.DMA((4, 4)),
        ],
        compiler_params=pltpu.CompilerParams(vmem_limit_bytes=24 * MIB),
        cost_estimate=pl.CostEstimate(
            flops=4 * count * width * half, bytes_accessed=4 * count * width, transcendentals=count
        ),
        name="block_state",
    )(in_hbm(series), in_hbm(weight), in_hbm(gain))


def prefix_kernel(pieces, out):
    total = jnp.zeros(pieces.shape[1:], jnp.float32)
    for k in range(pieces.shape[0]):
        rounded = total.astype(jnp.bfloat16)
        out[k] = rounded
        total = total + pieces[k].astype(jnp.float32)


def prefix(pieces):
    count, lines, lanes = pieces.shape
    return pl.pallas_call(
        prefix_kernel,
        in_specs=[pl.BlockSpec(memory_space=pltpu.VMEM)],
        out_specs=pl.BlockSpec(memory_space=pltpu.VMEM),
        out_shape=jax.ShapeDtypeStruct((count, lines, lanes), jnp.bfloat16),
        compiler_params=pltpu.CompilerParams(vmem_limit_bytes=4 * MIB),
        cost_estimate=pl.CostEstimate(
            flops=count * lines * lanes, bytes_accessed=6 * count * lines * lanes, transcendentals=0
        ),
        name="prefix",
    )(pieces)


def inside_kernel(series, gain, weight, queries_out, inside_out, queries_held, inside_held, sems):
    count, _ = series.shape
    own_rows, half = queries_held.shape
    heads = half // HD
    first_row = pl.multiple_of(lax.axis_index("head") * own_rows, own_rows)
    mine = normed_rows(series[pl.ds(first_row, own_rows), :], gain[...]).astype(jnp.bfloat16)
    normed = normed_rows(series[...], gain[...]).astype(jnp.bfloat16)
    row = lax.broadcasted_iota(jnp.int32, (own_rows, count), 0) + first_row
    causal = row >= lax.broadcasted_iota(jnp.int32, (own_rows, count), 1)
    queries, keys, values = (
        jnp.dot(rows, weight[k], preferred_element_type=jnp.float32).astype(jnp.bfloat16)
        for k, rows in ((0, mine), (1, normed), (2, normed))
    )
    queries_held[...] = queries
    keep_queries = pltpu.make_async_copy(queries_held, queries_out, sems.at[0])
    keep_queries.start()
    for n in range(heads):
        at = slice(n * HD, (n + 1) * HD)
        scores = lax.dot_general(
            queries[:, at],
            keys[:, at],
            (((1,), (1,)), ((), ())),
            preferred_element_type=jnp.float32,
        )
        scores = jnp.where(causal, scores, 0.0).astype(jnp.bfloat16)
        inside_held[:, at] = jnp.dot(scores, values[:, at], preferred_element_type=jnp.float32)
    keep_inside = pltpu.make_async_copy(inside_held, inside_out, sems.at[1])
    keep_inside.start()
    keep_queries.wait()
    keep_inside.wait()


def inside_block(series, gain, weight, own_rows):
    count, width = series.shape
    half = weight.shape[2]
    return pl.pallas_call(
        inside_kernel,
        in_specs=[pl.BlockSpec(memory_space=pltpu.VMEM)] * 3,
        out_specs=[pl.BlockSpec(memory_space=pl.ANY)] * 2,
        out_shape=[
            pltpu.HBM((own_rows, half), jnp.bfloat16),
            pltpu.HBM((own_rows, half), jnp.float32),
        ],
        scratch_shapes=[
            pltpu.VMEM((own_rows, half), jnp.bfloat16),
            pltpu.VMEM((own_rows, half), jnp.float32),
            pltpu.SemaphoreType.DMA((2,)),
        ],
        compiler_params=pltpu.CompilerParams(vmem_limit_bytes=24 * MIB),
        cost_estimate=pl.CostEstimate(
            flops=5 * count * width * half + 4 * own_rows * count * half,
            bytes_accessed=4 * count * width,
            transcendentals=0,
        ),
        name="inside_block",
    )(in_hbm(series), gain, in_hbm(weight))


def mix_kernel(
    queries_own,
    inside_own,
    queries_other,
    inside_other,
    state_own,
    state_other,
    out_own,
    out_other,
    series,
    gain,
    slots,
    ids,
    router,
    slot_column,
    residual_out,
    gate_out,
    send_out,
    queries_in,
    inside_in,
    weights_in,
    rows_in,
    residual_held,
    gate_held,
    sems,
):
    own_rows, _ = rows_in.shape
    half = out_own.shape[0]
    heads = half // HD
    first_row = pl.multiple_of(lax.axis_index("head") * own_rows, own_rows)
    fetches = [
        in_parts(queries_own, queries_in.at[0], sems.at[0], 2),
        in_parts(inside_own, inside_in.at[0], sems.at[1], 2),
        in_parts(out_own, weights_in.at[0], sems.at[2], 2),
        in_parts(queries_other, queries_in.at[1], sems.at[3], 2),
        in_parts(inside_other, inside_in.at[1], sems.at[4], 2),
        in_parts(out_other, weights_in.at[1], sems.at[5], 2),
        in_parts(series.at[pl.ds(first_row, own_rows)], rows_in, sems.at[6], 2),
    ]
    for some in fetches:
        for fetch in some:
            fetch.start()

    def arrived(k):
        for fetch in fetches[k]:
            fetch.wait()

    base = lax.axis_index(SEQ) * series.shape[0] + first_row + 1
    position = lax.broadcasted_iota(jnp.int32, (own_rows, HD), 0) + base
    unit = 1.0 / (position.astype(jnp.float32) * math.sqrt(HD))
    slot = lax.broadcasted_iota(jnp.int32, (send_out.shape[0], own_rows), 0)
    chosen = jnp.where(slot == slots[...], 1.0, 0.0).astype(jnp.bfloat16)
    total = None
    for part, state in ((0, state_own), (1, state_other)):
        arrived(3 * part)
        carried = [
            jnp.dot(
                queries_in[part, :, n * HD : (n + 1) * HD],
                state[n * HD : (n + 1) * HD, :],
                preferred_element_type=jnp.float32,
            )
            for n in range(heads)
        ]
        arrived(3 * part + 1)
        mixed = [
            ((inside_in[part, :, n * HD : (n + 1) * HD] + carried[n]) * unit).astype(jnp.bfloat16)
            for n in range(heads)
        ]
        arrived(3 * part + 2)
        added = jnp.dot(
            jnp.concatenate(mixed, axis=1), weights_in[part], preferred_element_type=jnp.float32
        )
        total = added if total is None else total + added
    arrived(6)
    total += rows_in[...].astype(jnp.float32)
    residual_held[...] = total
    keep_residual = in_parts(residual_held, residual_out, sems.at[7], 4)
    for keep in keep_residual:
        keep.start()
    normed = normed_rows(total, gain[...]).astype(jnp.bfloat16)
    logits = jnp.dot(normed, router[...], preferred_element_type=jnp.float32)
    expert = lax.broadcasted_iota(jnp.int32, logits.shape, 1)
    logit = jnp.sum(jnp.where(expert == ids[...], logits, 0.0), axis=1, keepdims=True)
    gate_held[...] = jnp.broadcast_to(jax.nn.sigmoid(logit), gate_held.shape)
    middle = send_out.shape[0] // 2
    send_out[:middle, :] = jnp.dot(
        chosen[:middle], normed, preferred_element_type=jnp.float32
    ).astype(jnp.bfloat16)
    keep_gate = pltpu.make_async_copy(gate_held, gate_out, sems.at[8, 0])
    keep_gate.start()
    send_out[middle:, :] = jnp.dot(
        chosen[middle:], normed, preferred_element_type=jnp.float32
    ).astype(jnp.bfloat16)
    for keep in keep_residual:
        keep.wait()
    keep_gate.wait()


def mix_heads(
    part_own,
    part_other,
    state_own,
    state_other,
    out_own,
    out_other,
    series,
    gain,
    slots,
    ids,
    router,
    slot_column,
    slot_count,
):
    own_rows = slots.shape[1]
    width = series.shape[1]
    half = out_own.shape[0]
    anywhere = pl.BlockSpec(memory_space=pl.ANY)
    local = pl.BlockSpec(memory_space=pltpu.VMEM)
    return pl.pallas_call(
        mix_kernel,
        in_specs=[anywhere] * 4 + [local] * 2 + [anywhere] * 3 + [local] * 4 + [anywhere],
        out_specs=[anywhere, anywhere, local],
        out_shape=[
            pltpu.HBM((own_rows, width), jnp.float32),
            pltpu.HBM((own_rows, HD), jnp.float32),
            jax.ShapeDtypeStruct((slot_count, width), jnp.bfloat16),
        ],
        scratch_shapes=[
            pltpu.VMEM((2, own_rows, half), jnp.bfloat16),
            pltpu.VMEM((2, own_rows, half), jnp.float32),
            pltpu.VMEM((2, half, width), jnp.bfloat16),
            pltpu.VMEM((own_rows, width), jnp.bfloat16),
            pltpu.VMEM((own_rows, width), jnp.float32),
            pltpu.VMEM((own_rows, HD), jnp.float32),
            pltpu.SemaphoreType.DMA((9, 4)),
        ],
        compiler_params=pltpu.CompilerParams(vmem_limit_bytes=24 * MIB),
        cost_estimate=pl.CostEstimate(
            flops=2 * own_rows * width * (width + 2 * HD + slot_count),
            bytes_accessed=12 * own_rows * width,
            transcendentals=own_rows,
        ),
        name="mix_heads",
    )(
        *(in_hbm(array) for array in (*part_own, *part_other)),
        state_own,
        state_other,
        in_hbm(out_own),
        in_hbm(out_other),
        in_hbm(series),
        gain,
        slots,
        ids,
        router,
        slot_column,
    )


def combine_kernel(returned, residual, gate, slots, out, residual_in, gate_in, held, sems):
    own_rows, width = residual_in.shape
    parts = 4
    fetches = in_parts(residual, residual_in, sems.at[0], parts)
    fetch_gate = pltpu.make_async_copy(gate, gate_in, sems.at[1, 0])
    fetch_gate.start()
    for fetch in fetches:
        fetch.start()
    leave = in_parts(held, out, sems.at[2], parts)
    slot = lax.broadcasted_iota(jnp.int32, (own_rows, returned.shape[0]), 1)
    chosen = jnp.where(slot == slots[...], 1.0, 0.0).astype(jnp.bfloat16)
    routed = jnp.dot(chosen, returned[...], preferred_element_type=jnp.float32)
    fetch_gate.wait()
    size = own_rows // parts
    for k in range(parts):
        at = slice(k * size, (k + 1) * size)
        weight = jnp.concatenate([gate_in[at, :]] * (width // HD), axis=1)
        fetches[k].wait()
        held[at, :] = (residual_in[at, :] + weight * routed[at]).astype(jnp.bfloat16)
        leave[k].start()
    for copy in leave:
        copy.wait()


def combine(returned, residual, gate, slots):
    own_rows, width = residual.shape
    anywhere = pl.BlockSpec(memory_space=pl.ANY)
    local = pl.BlockSpec(memory_space=pltpu.VMEM)
    return pl.pallas_call(
        combine_kernel,
        in_specs=[local, anywhere, anywhere, local],
        out_specs=anywhere,
        out_shape=pltpu.HBM((own_rows, width), jnp.bfloat16),
        scratch_shapes=[
            pltpu.VMEM((own_rows, width), jnp.float32),
            pltpu.VMEM((own_rows, HD), jnp.float32),
            pltpu.VMEM((own_rows, width), jnp.bfloat16),
            pltpu.SemaphoreType.DMA((3, 4)),
        ],
        compiler_params=pltpu.CompilerParams(vmem_limit_bytes=24 * MIB),
        cost_estimate=pl.CostEstimate(
            flops=2 * own_rows * width * returned.shape[0],
            bytes_accessed=10 * own_rows * width,
            transcendentals=0,
        ),
        name="combine",
    )(returned, in_hbm(residual), in_hbm(gate), slots)


def on_device(
    series,
    norm_attn,
    qkv_weight,
    out_weight,
    norm_moe,
    router_weight,
    expert_ids,
    gate_weight,
    up_weight,
    down_weight,
):
    width = series.shape[2]
    head_count = lax.axis_size("head")
    seq_size = lax.axis_size(SEQ)
    own_rows = series.shape[1] // head_count

    qkv_own = jnp.moveaxis(qkv_weight, 1, 0)
    own_expert = (gate_weight[0], up_weight[0], down_weight[0])
    qkv_other = from_partner(qkv_own)
    out_other = from_partner(out_weight)
    other_expert = tuple(from_partner(w) for w in own_expert)

    state = block_state(series[0], qkv_own, norm_attn)
    pieces = exchange(state.reshape(seq_size, state.shape[0] // seq_size, HD), SEQ)
    state_own = exchange(prefix(pieces), SEQ)
    state_other = from_partner(state_own)
    part_own = inside_block(series[0], norm_attn, qkv_own, own_rows)
    part_other = inside_block(series[0], norm_attn, qkv_other, own_rows)

    route_ids = expert_ids[0, :, 0]
    expert_count = router_weight.shape[1]
    capacity = 2 * own_rows // expert_count
    earlier_row = jnp.arange(own_rows)[None, :] < jnp.arange(own_rows)[:, None]
    same_expert = route_ids[:, None] == route_ids[None, :]
    slot_rank = jnp.sum(jnp.logical_and(same_expert, earlier_row), axis=1)
    slot_index = route_ids * capacity + slot_rank

    slots = slot_index[None, :]
    slot_column = slot_index[:, None]
    residual, gate, send_buffer = mix_heads(
        part_own,
        part_other,
        state_own.reshape(state.shape),
        state_other.reshape(state.shape),
        out_weight,
        out_other,
        series[0],
        norm_moe,
        slots,
        route_ids[:, None],
        router_weight,
        slot_column,
        expert_count * capacity,
    )
    received = exchange(send_buffer.reshape(expert_count, capacity, width), SEQ_DP)

    expert_out = expert_of(received.reshape(-1, width), own_expert, other_expert)
    returned = exchange(expert_out.reshape(received.shape), SEQ_DP)
    layer_out = combine(returned.reshape(send_buffer.shape), residual, gate, slot_column)
    return layer_out[None]


def solution(mesh):
    split = Mesh(
        mesh.devices.reshape(8, 4, mesh.shape["head"], mesh.shape["dp"]),
        ("seq_0", "seq_1", "head", "dp"),
    )
    placed = (
        P("dp", SEQ, None),
        P(),
        P(None, None, "head"),
        P("head", None),
        P(),
        P(),
        P("dp", SEQ_HEAD, None),
        P(SEQ_DP, None, "head"),
        P(SEQ_DP, None, "head"),
        P(SEQ_DP, "head", None),
    )

    return jax.shard_map(
        on_device, mesh=split, in_specs=placed, out_specs=P("dp", SEQ_HEAD, None), check_vma=False
    )
```

```python
import math

import jax
import jax.numpy as jnp
from jax import lax
from jax.experimental import pallas as pl
from jax.experimental.pallas import tpu as pltpu
from jax.sharding import Mesh
from jax.sharding import PartitionSpec as P


HD = 128
SEQ = ("seq_0", "seq_1")
SEQ_DP = ("seq_0", "seq_1", "dp")
SEQ_HEAD = ("seq_0", "seq_1", "head")
NORM_EPS = 1e-06
FF_BLOCK = 512
MIB = 1024 * 1024


def from_partner(shard):
    return lax.ppermute(shard, "head", [(0, 1), (1, 0)])


def exchange(pieces, axes):
    return lax.all_to_all(pieces, axes, split_axis=0, concat_axis=0, tiled=True)


def expert_kernel(rows, gate_a, up_a, down_a, gate_b, up_b, down_b, out, gate, up, down, total, sems):
    blocks = gate.shape[0]
    own_blocks = blocks // 2
    first = FF_BLOCK // 2

    def copies(k):
        gates, ups, downs = (gate_a, up_a, down_a) if k < own_blocks else (gate_b, up_b, down_b)
        base = (k % own_blocks) * FF_BLOCK
        spans = ((0, first), (first, first)) if k == 0 else ((0, FF_BLOCK),)
        for n, (at, size) in enumerate(spans):
            row = 0 if k == 0 and n == 0 else k + 1
            to, source = pl.ds(at, size), pl.ds(base + at, size)
            yield pltpu.make_async_copy(gates.at[:, source], gate.at[k, :, to], sems.at[row, 0])
            yield pltpu.make_async_copy(ups.at[:, source], up.at[k, :, to], sems.at[row, 1])
            yield pltpu.make_async_copy(downs.at[source, :], down.at[k, to, :], sems.at[row, 2])

    started = [list(copies(k)) for k in range(blocks)]
    for some in started:
        for copy in some:
            copy.start()

    def part(gates, ups, downs):
        x = rows[...]
        g = jnp.dot(x, gates, preferred_element_type=jnp.float32)
        u = jnp.dot(x, ups, preferred_element_type=jnp.float32)
        hidden = (g * (0.5 + 0.5 * jnp.tanh(0.5 * g)) * u).astype(jnp.bfloat16)
        return jnp.dot(hidden, downs, preferred_element_type=jnp.float32)

    for copy in started[0][:3]:
        copy.wait()
    total[...] = part(gate[0, :, :first], up[0, :, :first], down[0, :first, :])
    for copy in started[0][3:]:
        copy.wait()
    total[...] += part(gate[0, :, first:], up[0, :, first:], down[0, first:, :])

    def step(k, carry):
        whole = pl.ds(0, FF_BLOCK)
        pltpu.make_async_copy(gate_a.at[:, whole], gate.at[k], sems.at[k + 1, 0]).wait()
        pltpu.make_async_copy(up_a.at[:, whole], up.at[k], sems.at[k + 1, 1]).wait()
        pltpu.make_async_copy(down_a.at[whole, :], down.at[k], sems.at[k + 1, 2]).wait()
        total[...] += part(gate[k], up[k], down[k])
        return carry

    lax.fori_loop(1, blocks, step, 0)
    out[...] = total[...].astype(out.dtype)


def expert_of(rows, own, partner):
    count, width = rows.shape
    units = own[0].shape[1]
    blocks = 2 * units // FF_BLOCK
    local = pl.BlockSpec(memory_space=pltpu.VMEM)
    return pl.pallas_call(
        expert_kernel,
        in_specs=[local] + [pl.BlockSpec(memory_space=pl.ANY)] * 6,
        out_specs=local,
        out_shape=jax.ShapeDtypeStruct((count, width), jnp.bfloat16),
        scratch_shapes=[
            pltpu.VMEM((blocks, width, FF_BLOCK), jnp.bfloat16),
            pltpu.VMEM((blocks, width, FF_BLOCK), jnp.bfloat16),
            pltpu.VMEM((blocks, FF_BLOCK, width), jnp.bfloat16),
            pltpu.VMEM((count, width), jnp.float32),
            pltpu.SemaphoreType.DMA((blocks + 1, 3)),
        ],
        compiler_params=pltpu.CompilerParams(vmem_limit_bytes=36 * MIB),
        cost_estimate=pl.CostEstimate(
            flops=2 * count * width * units * 6,
            bytes_accessed=12 * width * units,
            transcendentals=2 * count * units,
        ),
        name="expert_mlp",
    )(rows, *(in_hbm(w) for w in own), *(in_hbm(w) for w in partner))


def in_parts(source, target, sems, parts):
    size = source.shape[0] // parts
    return [
        pltpu.make_async_copy(
            source.at[pl.ds(k * size, size)], target.at[pl.ds(k * size, size)], sems.at[k]
        )
        for k in range(parts)
    ]


def in_hbm(array):
    return pltpu.with_memory_space_constraint(array, pltpu.HBM)


def in_vmem(array):
    return pltpu.with_memory_space_constraint(array, pltpu.VMEM)


def normed_rows(rows, gain):
    x = rows.astype(jnp.float32)
    mean = jnp.sum(x * x, axis=-1, keepdims=True) * (1.0 / x.shape[1])
    return x * lax.rsqrt(mean + NORM_EPS) * gain.reshape(1, -1)


def state_kernel(
    series, weight, gain, state_out, normed_out, rows, table, gain_in, sems
):
    half = table.shape[2]
    fetches = [
        in_parts(series, rows, sems.at[0], 4),
        in_parts(weight.at[1], table.at[0], sems.at[1], 4),
        in_parts(weight.at[2], table.at[1], sems.at[2], 4),
    ]
    fetch_gain = pltpu.make_async_copy(gain, gain_in, sems.at[3, 0])
    for fetch in fetches[0]:
        fetch.start()
    fetch_gain.start()
    for some in fetches[1:]:
        for fetch in some:
            fetch.start()
    for fetch in fetches[0]:
        fetch.wait()
    fetch_gain.wait()
    normed = normed_rows(rows[...], gain_in[...]).astype(jnp.bfloat16)
    normed_out[...] = normed
    for fetch in fetches[1]:
        fetch.wait()
    keys = jnp.dot(normed, table[0], preferred_element_type=jnp.float32).astype(jnp.bfloat16)
    for fetch in fetches[2]:
        fetch.wait()
    values = jnp.dot(normed, table[1], preferred_element_type=jnp.float32).astype(jnp.bfloat16)
    heads = half // HD
    for n in range(heads):
        at = slice(n * HD, (n + 1) * HD)
        state_out[at, :] = lax.dot_general(
            keys[:, at], values[:, at], (((0,), (0,)), ((), ())), preferred_element_type=jnp.float32
        ).astype(jnp.bfloat16)
    state_out[heads * HD :, :] = jnp.zeros((HD, HD), jnp.bfloat16)


def block_state(series, weight, gain):
    count, width = series.shape
    half = weight.shape[2]
    return pl.pallas_call(
        state_kernel,
        in_specs=[
            pl.BlockSpec(memory_space=pl.ANY),
            pl.BlockSpec(memory_space=pl.ANY),
            pl.BlockSpec(memory_space=pl.ANY),
        ],
        out_specs=[pl.BlockSpec(memory_space=pltpu.VMEM)] * 2,
        out_shape=[
            jax.ShapeDtypeStruct((half + HD, HD), jnp.bfloat16),
            pltpu.VMEM((count, width), jnp.bfloat16),
        ],
        scratch_shapes=[
            pltpu.VMEM((count, width), jnp.bfloat16),
            pltpu.VMEM((2, width, half), jnp.bfloat16),
            pltpu.VMEM((width,), jnp.float32),
            pltpu.SemaphoreType.DMA((4, 4)),
        ],
        compiler_params=pltpu.CompilerParams(vmem_limit_bytes=24 * MIB),
        cost_estimate=pl.CostEstimate(
            flops=4 * count * width * half, bytes_accessed=4 * count * width, transcendentals=count
        ),
        name="block_state",
    )(in_hbm(series), in_hbm(weight), in_hbm(gain))


def prefix_kernel(pieces, out):
    total = jnp.zeros(pieces.shape[1:], jnp.float32)
    for k in range(pieces.shape[0]):
        rounded = total.astype(jnp.bfloat16)
        out[k] = rounded
        total = total + pieces[k].astype(jnp.float32)


def prefix(pieces):
    count, lines, lanes = pieces.shape
    return pl.pallas_call(
        prefix_kernel,
        in_specs=[pl.BlockSpec(memory_space=pltpu.VMEM)],
        out_specs=pl.BlockSpec(memory_space=pltpu.VMEM),
        out_shape=jax.ShapeDtypeStruct((count, lines, lanes), jnp.bfloat16),
        compiler_params=pltpu.CompilerParams(vmem_limit_bytes=4 * MIB),
        cost_estimate=pl.CostEstimate(
            flops=count * lines * lanes, bytes_accessed=6 * count * lines * lanes, transcendentals=0
        ),
        name="prefix",
    )(pieces)


def inside_kernel(normed, weight, queries_out, inside_out, table, sems):
    count, _ = normed.shape
    own_rows, half = queries_out.shape
    heads = half // HD
    fetches = [in_parts(weight.at[k], table.at[k], sems.at[k], 2) for k in range(3)]
    for k in (1, 2, 0):
        for fetch in fetches[k]:
            fetch.start()
    first_row = pl.multiple_of(lax.axis_index("head") * own_rows, own_rows)
    row = lax.broadcasted_iota(jnp.int32, (own_rows, count), 0) + first_row
    causal = row >= lax.broadcasted_iota(jnp.int32, (own_rows, count), 1)

    def project(source, k):
        for fetch in fetches[k]:
            fetch.wait()
        return jnp.dot(source, table[k], preferred_element_type=jnp.float32).astype(jnp.bfloat16)

    keys, values = project(normed[...], 1), project(normed[...], 2)
    queries = project(normed[pl.ds(first_row, own_rows), :], 0)
    queries_out[...] = queries
    for n in range(heads):
        at = slice(n * HD, (n + 1) * HD)
        scores = lax.dot_general(
            queries[:, at],
            keys[:, at],
            (((1,), (1,)), ((), ())),
            preferred_element_type=jnp.float32,
        )
        scores = jnp.where(causal, scores, 0.0).astype(jnp.bfloat16)
        inside_out[:, at] = jnp.dot(scores, values[:, at], preferred_element_type=jnp.float32)


def inside_block(normed, weight, own_rows):
    count, width = normed.shape
    half = weight.shape[2]
    local = pl.BlockSpec(memory_space=pltpu.VMEM)
    return pl.pallas_call(
        inside_kernel,
        in_specs=[local, pl.BlockSpec(memory_space=pl.ANY)],
        out_specs=[local] * 2,
        out_shape=[
            pltpu.VMEM((own_rows, half), jnp.bfloat16),
            pltpu.VMEM((own_rows, half), jnp.float32),
        ],
        scratch_shapes=[
            pltpu.VMEM((3, width, half), jnp.bfloat16),
            pltpu.SemaphoreType.DMA((3, 2)),
        ],
        compiler_params=pltpu.CompilerParams(vmem_limit_bytes=24 * MIB),
        cost_estimate=pl.CostEstimate(
            flops=5 * count * width * half + 4 * own_rows * count * half,
            bytes_accessed=4 * count * width,
            transcendentals=0,
        ),
        name="inside_block",
    )(in_vmem(normed), in_hbm(weight))


def mix_kernel(
    queries_own,
    inside_own,
    queries_other,
    inside_other,
    state_own,
    state_other,
    out_own,
    out_other,
    series,
    gain,
    slots,
    ids,
    router,
    slot_column,
    residual_out,
    send_out,
    weights_in,
    rows_in,
    router_in,
    sems,
):
    own_rows, width = rows_in.shape
    half = out_own.shape[0]
    heads = half // HD
    first_row = pl.multiple_of(lax.axis_index("head") * own_rows, own_rows)
    fetches = [
        in_parts(out_own, weights_in.at[0], sems.at[0], 2),
        in_parts(out_other, weights_in.at[1], sems.at[1], 2),
        in_parts(series.at[pl.ds(first_row, own_rows)], rows_in, sems.at[2], 2),
        in_parts(router, router_in, sems.at[3], 1),
    ]
    for some in fetches:
        for fetch in some:
            fetch.start()

    def arrived(k):
        for fetch in fetches[k]:
            fetch.wait()

    base = lax.axis_index(SEQ) * series.shape[0] + first_row + 1
    position = lax.broadcasted_iota(jnp.int32, (own_rows, HD), 0) + base
    unit = 1.0 / (position.astype(jnp.float32) * math.sqrt(HD))
    slot = lax.broadcasted_iota(jnp.int32, (send_out.shape[0], own_rows), 0)
    chosen = jnp.where(slot == slots[...], 1.0, 0.0).astype(jnp.bfloat16)
    total = None
    for part, queries, inside, state in (
        (0, queries_own, inside_own, state_own),
        (1, queries_other, inside_other, state_other),
    ):
        mixed = []
        for n in range(heads):
            at = slice(n * HD, (n + 1) * HD)
            carried = jnp.dot(queries[:, at], state[at, :], preferred_element_type=jnp.float32)
            mixed.append(((inside[:, at] + carried) * unit).astype(jnp.bfloat16))
        arrived(part)
        added = jnp.dot(
            jnp.concatenate(mixed, axis=1), weights_in[part], preferred_element_type=jnp.float32
        )
        total = added if total is None else total + added
    arrived(2)
    total += rows_in[...].astype(jnp.float32)
    residual_out[:, :width] = total
    normed = normed_rows(total, gain[...]).astype(jnp.bfloat16)
    send_out[...] = jnp.dot(chosen, normed, preferred_element_type=jnp.float32).astype(
        jnp.bfloat16
    )
    arrived(3)
    logits = jnp.dot(normed, router_in[...], preferred_element_type=jnp.float32)
    expert = lax.broadcasted_iota(jnp.int32, logits.shape, 1)
    logit = jnp.sum(jnp.where(expert == ids[...], logits, 0.0), axis=1, keepdims=True)
    residual_out[:, width:] = jnp.broadcast_to(jax.nn.sigmoid(logit), (own_rows, HD))


def mix_heads(
    part_own,
    part_other,
    state_own,
    state_other,
    out_own,
    out_other,
    series,
    gain,
    slots,
    ids,
    router,
    slot_column,
    slot_count,
):
    own_rows = slots.shape[1]
    width = series.shape[1]
    half = out_own.shape[0]
    anywhere = pl.BlockSpec(memory_space=pl.ANY)
    local = pl.BlockSpec(memory_space=pltpu.VMEM)
    return pl.pallas_call(
        mix_kernel,
        in_specs=[local] * 6 + [anywhere] * 3 + [local] * 3 + [anywhere] * 2,
        out_specs=[local] * 2,
        out_shape=[
            pltpu.VMEM((own_rows, width + HD), jnp.float32),
            jax.ShapeDtypeStruct((slot_count, width), jnp.bfloat16),
        ],
        scratch_shapes=[
            pltpu.VMEM((2, half, width), jnp.bfloat16),
            pltpu.VMEM((own_rows, width), jnp.bfloat16),
            pltpu.VMEM(router.shape, jnp.bfloat16),
            pltpu.SemaphoreType.DMA((4, 2)),
        ],
        compiler_params=pltpu.CompilerParams(vmem_limit_bytes=24 * MIB),
        cost_estimate=pl.CostEstimate(
            flops=2 * own_rows * width * (width + 2 * HD + slot_count),
            bytes_accessed=12 * own_rows * width,
            transcendentals=own_rows,
        ),
        name="mix_heads",
    )(
        *(in_vmem(array) for array in (*part_own, *part_other)),
        state_own,
        state_other,
        in_hbm(out_own),
        in_hbm(out_other),
        in_hbm(series),
        gain,
        slots,
        ids,
        in_hbm(router),
        slot_column,
    )


def combine_kernel(returned, residual, slots, out, held, sems):
    own_rows, width = held.shape
    parts = 4
    leave = in_parts(held, out, sems, parts)
    slot = lax.broadcasted_iota(jnp.int32, (own_rows, returned.shape[0]), 1)
    chosen = jnp.where(slot == slots[...], 1.0, 0.0).astype(jnp.bfloat16)
    size = own_rows // parts
    for k in range(parts):
        at = slice(k * size, (k + 1) * size)
        routed = jnp.dot(chosen[at], returned[...], preferred_element_type=jnp.float32)
        weight = jnp.concatenate([residual[at, width:]] * (width // HD), axis=1)
        held[at, :] = (residual[at, :width] + weight * routed).astype(jnp.bfloat16)
        leave[k].start()
    for copy in leave:
        copy.wait()


def combine(returned, residual, slots):
    own_rows, width = residual.shape[0], returned.shape[1]
    anywhere = pl.BlockSpec(memory_space=pl.ANY)
    local = pl.BlockSpec(memory_space=pltpu.VMEM)
    return pl.pallas_call(
        combine_kernel,
        in_specs=[local] * 3,
        out_specs=anywhere,
        out_shape=pltpu.HBM((own_rows, width), jnp.bfloat16),
        scratch_shapes=[
            pltpu.VMEM((own_rows, width), jnp.bfloat16),
            pltpu.SemaphoreType.DMA((4,)),
        ],
        compiler_params=pltpu.CompilerParams(vmem_limit_bytes=24 * MIB),
        cost_estimate=pl.CostEstimate(
            flops=2 * own_rows * width * returned.shape[0],
            bytes_accessed=10 * own_rows * width,
            transcendentals=0,
        ),
        name="combine",
    )(returned, in_vmem(residual), slots)


def on_device(
    series,
    norm_attn,
    qkv_weight,
    out_weight,
    norm_moe,
    router_weight,
    expert_ids,
    gate_weight,
    up_weight,
    down_weight,
):
    width = series.shape[2]
    head_count = lax.axis_size("head")
    seq_size = lax.axis_size(SEQ)
    own_rows = series.shape[1] // head_count

    qkv_own = jnp.moveaxis(qkv_weight, 1, 0)
    own_expert = (gate_weight[0], up_weight[0], down_weight[0])
    qkv_other = from_partner(qkv_own)
    out_other = from_partner(out_weight)
    other_expert = tuple(from_partner(w) for w in own_expert)

    state, normed_in = block_state(series[0], qkv_own, norm_attn)
    pieces = exchange(state.reshape(seq_size, state.shape[0] // seq_size, HD), SEQ)
    state_own = exchange(prefix(pieces), SEQ)
    state_other = from_partner(state_own)
    part_own = inside_block(normed_in, qkv_own, own_rows)
    part_other = inside_block(normed_in, qkv_other, own_rows)

    route_ids = expert_ids[0, :, 0]
    expert_count = router_weight.shape[1]
    capacity = 2 * own_rows // expert_count
    earlier_row = jnp.arange(own_rows)[None, :] < jnp.arange(own_rows)[:, None]
    same_expert = route_ids[:, None] == route_ids[None, :]
    slot_rank = jnp.sum(jnp.logical_and(same_expert, earlier_row), axis=1)
    slot_index = route_ids * capacity + slot_rank

    slots = slot_index[None, :]
    slot_column = slot_index[:, None]
    residual, send_buffer = mix_heads(
        part_own,
        part_other,
        state_own.reshape(state.shape),
        state_other.reshape(state.shape),
        out_weight,
        out_other,
        series[0],
        norm_moe,
        slots,
        route_ids[:, None],
        router_weight,
        slot_column,
        expert_count * capacity,
    )
    received = exchange(send_buffer.reshape(expert_count, capacity, width), SEQ_DP)

    expert_out = expert_of(received.reshape(-1, width), own_expert, other_expert)
    returned = exchange(expert_out.reshape(received.shape), SEQ_DP)
    layer_out = combine(returned.reshape(send_buffer.shape), residual, slot_column)
    return layer_out[None]


def solution(mesh):
    split = Mesh(
        mesh.devices.reshape(8, 4, mesh.shape["head"], mesh.shape["dp"]),
        ("seq_0", "seq_1", "head", "dp"),
    )
    placed = (
        P("dp", SEQ, None),
        P(),
        P(None, None, "head"),
        P("head", None),
        P(),
        P(),
        P("dp", SEQ_HEAD, None),
        P(SEQ_DP, None, "head"),
        P(SEQ_DP, None, "head"),
        P(SEQ_DP, "head", None),
    )

    return jax.shard_map(
        on_device, mesh=split, in_specs=placed, out_specs=P("dp", SEQ_HEAD, None), check_vma=False
    )
```

```python
import math

import jax
import jax.numpy as jnp
from jax import lax
from jax.experimental import pallas as pl
from jax.experimental.pallas import tpu as pltpu
from jax.sharding import Mesh
from jax.sharding import PartitionSpec as P


HD = 128
SEQ = ("seq_0", "seq_1")
SEQ_DP = ("seq_0", "seq_1", "dp")
SEQ_HEAD = ("seq_0", "seq_1", "head")
NORM_EPS = 1e-06
FF_BLOCK = 512
MIB = 1024 * 1024


def from_partner(shard):
    return lax.ppermute(shard, "head", [(0, 1), (1, 0)])


def exchange(pieces, axes):
    return lax.all_to_all(pieces, axes, split_axis=0, concat_axis=0, tiled=True)


def expert_kernel(rows, gate_a, up_a, down_a, gate_b, up_b, down_b, out, gate, up, down, total, sems):
    blocks = gate.shape[0]
    own_blocks = blocks // 2
    first = FF_BLOCK // 2

    def copies(k):
        gates, ups, downs = (gate_a, up_a, down_a) if k < own_blocks else (gate_b, up_b, down_b)
        base = (k % own_blocks) * FF_BLOCK
        spans = ((0, first), (first, first)) if k == 0 else ((0, FF_BLOCK),)
        for n, (at, size) in enumerate(spans):
            row = 0 if k == 0 and n == 0 else k + 1
            to, source = pl.ds(at, size), pl.ds(base + at, size)
            yield pltpu.make_async_copy(gates.at[:, source], gate.at[k, :, to], sems.at[row, 0])
            yield pltpu.make_async_copy(ups.at[:, source], up.at[k, :, to], sems.at[row, 1])
            yield pltpu.make_async_copy(downs.at[source, :], down.at[k, to, :], sems.at[row, 2])

    started = [list(copies(k)) for k in range(blocks)]
    for some in started:
        for copy in some:
            copy.start()

    def part(gates, ups, downs):
        x = rows[...]
        g = jnp.dot(x, gates, preferred_element_type=jnp.float32)
        u = jnp.dot(x, ups, preferred_element_type=jnp.float32)
        hidden = (g * (0.5 + 0.5 * jnp.tanh(0.5 * g)) * u).astype(jnp.bfloat16)
        return jnp.dot(hidden, downs, preferred_element_type=jnp.float32)

    for copy in started[0][:3]:
        copy.wait()
    total[...] = part(gate[0, :, :first], up[0, :, :first], down[0, :first, :])
    for copy in started[0][3:]:
        copy.wait()
    total[...] += part(gate[0, :, first:], up[0, :, first:], down[0, first:, :])

    def step(k, carry):
        whole = pl.ds(0, FF_BLOCK)
        pltpu.make_async_copy(gate_a.at[:, whole], gate.at[k], sems.at[k + 1, 0]).wait()
        pltpu.make_async_copy(up_a.at[:, whole], up.at[k], sems.at[k + 1, 1]).wait()
        pltpu.make_async_copy(down_a.at[whole, :], down.at[k], sems.at[k + 1, 2]).wait()
        total[...] += part(gate[k], up[k], down[k])
        return carry

    lax.fori_loop(1, blocks, step, 0)
    out[...] = total[...].astype(out.dtype)


def expert_of(rows, own, partner):
    count, width = rows.shape
    units = own[0].shape[1]
    blocks = 2 * units // FF_BLOCK
    local = pl.BlockSpec(memory_space=pltpu.VMEM)
    return pl.pallas_call(
        expert_kernel,
        in_specs=[local] + [pl.BlockSpec(memory_space=pl.ANY)] * 6,
        out_specs=local,
        out_shape=jax.ShapeDtypeStruct((count, width), jnp.bfloat16),
        scratch_shapes=[
            pltpu.VMEM((blocks, width, FF_BLOCK), jnp.bfloat16),
            pltpu.VMEM((blocks, width, FF_BLOCK), jnp.bfloat16),
            pltpu.VMEM((blocks, FF_BLOCK, width), jnp.bfloat16),
            pltpu.VMEM((count, width), jnp.float32),
            pltpu.SemaphoreType.DMA((blocks + 1, 3)),
        ],
        compiler_params=pltpu.CompilerParams(vmem_limit_bytes=36 * MIB),
        cost_estimate=pl.CostEstimate(
            flops=2 * count * width * units * 6,
            bytes_accessed=12 * width * units,
            transcendentals=2 * count * units,
        ),
        name="expert_mlp",
    )(rows, *(in_hbm(w) for w in own), *(in_hbm(w) for w in partner))


def in_parts(source, target, sems, parts):
    size = source.shape[0] // parts
    return [
        pltpu.make_async_copy(
            source.at[pl.ds(k * size, size)], target.at[pl.ds(k * size, size)], sems.at[k]
        )
        for k in range(parts)
    ]


def in_hbm(array):
    return pltpu.with_memory_space_constraint(array, pltpu.HBM)


def in_vmem(array):
    return pltpu.with_memory_space_constraint(array, pltpu.VMEM)


def normed_rows(rows, gain):
    x = rows.astype(jnp.float32)
    mean = jnp.sum(x * x, axis=-1, keepdims=True) * (1.0 / x.shape[1])
    return x * lax.rsqrt(mean + NORM_EPS) * gain.reshape(1, -1)


def state_kernel(
    series, weight, gain, state_out, normed_out, rows, table, gain_in, sems
):
    half = table.shape[2]
    fetches = [
        in_parts(series, rows, sems.at[0], 4),
        in_parts(weight.at[1], table.at[0], sems.at[1], 4),
        in_parts(weight.at[2], table.at[1], sems.at[2], 4),
    ]
    fetch_gain = pltpu.make_async_copy(gain, gain_in, sems.at[3, 0])
    for fetch in fetches[0]:
        fetch.start()
    fetch_gain.start()
    for some in fetches[1:]:
        for fetch in some:
            fetch.start()
    fetch_gain.wait()
    size = rows.shape[0] // len(fetches[0])
    for k, fetch in enumerate(fetches[0]):
        at = slice(k * size, (k + 1) * size)
        fetch.wait()
        normed_out[at, :] = normed_rows(rows[at, :], gain_in[...]).astype(jnp.bfloat16)
    normed = normed_out[...]
    for fetch in fetches[1]:
        fetch.wait()
    keys = jnp.dot(normed, table[0], preferred_element_type=jnp.float32).astype(jnp.bfloat16)
    for fetch in fetches[2]:
        fetch.wait()
    values = jnp.dot(normed, table[1], preferred_element_type=jnp.float32).astype(jnp.bfloat16)
    heads = half // HD
    for n in range(heads):
        at = slice(n * HD, (n + 1) * HD)
        state_out[at, :] = lax.dot_general(
            keys[:, at], values[:, at], (((0,), (0,)), ((), ())), preferred_element_type=jnp.float32
        ).astype(jnp.bfloat16)
    state_out[heads * HD :, :] = jnp.zeros((HD, HD), jnp.bfloat16)


def block_state(series, weight, gain):
    count, width = series.shape
    half = weight.shape[2]
    return pl.pallas_call(
        state_kernel,
        in_specs=[
            pl.BlockSpec(memory_space=pl.ANY),
            pl.BlockSpec(memory_space=pl.ANY),
            pl.BlockSpec(memory_space=pl.ANY),
        ],
        out_specs=[pl.BlockSpec(memory_space=pltpu.VMEM)] * 2,
        out_shape=[
            jax.ShapeDtypeStruct((half + HD, HD), jnp.bfloat16),
            pltpu.VMEM((count, width), jnp.bfloat16),
        ],
        scratch_shapes=[
            pltpu.VMEM((count, width), jnp.bfloat16),
            pltpu.VMEM((2, width, half), jnp.bfloat16),
            pltpu.VMEM((width,), jnp.float32),
            pltpu.SemaphoreType.DMA((4, 4)),
        ],
        compiler_params=pltpu.CompilerParams(vmem_limit_bytes=24 * MIB),
        cost_estimate=pl.CostEstimate(
            flops=4 * count * width * half, bytes_accessed=4 * count * width, transcendentals=count
        ),
        name="block_state",
    )(in_hbm(series), in_hbm(weight), in_hbm(gain))


def prefix_kernel(pieces, out):
    total = jnp.zeros(pieces.shape[1:], jnp.float32)
    for k in range(pieces.shape[0]):
        rounded = total.astype(jnp.bfloat16)
        out[k] = rounded
        total = total + pieces[k].astype(jnp.float32)


def prefix(pieces):
    count, lines, lanes = pieces.shape
    return pl.pallas_call(
        prefix_kernel,
        in_specs=[pl.BlockSpec(memory_space=pltpu.VMEM)],
        out_specs=pl.BlockSpec(memory_space=pltpu.VMEM),
        out_shape=jax.ShapeDtypeStruct((count, lines, lanes), jnp.bfloat16),
        compiler_params=pltpu.CompilerParams(vmem_limit_bytes=4 * MIB),
        cost_estimate=pl.CostEstimate(
            flops=count * lines * lanes, bytes_accessed=6 * count * lines * lanes, transcendentals=0
        ),
        name="prefix",
    )(pieces)


def inside_kernel(normed, weight, queries_out, inside_out, table, sems):
    count, _ = normed.shape
    own_rows, half = queries_out.shape
    heads = half // HD
    fetches = [in_parts(weight.at[k], table.at[k], sems.at[k], 2) for k in range(3)]
    for k in (1, 2, 0):
        for fetch in fetches[k]:
            fetch.start()
    first_row = pl.multiple_of(lax.axis_index("head") * own_rows, own_rows)
    row = lax.broadcasted_iota(jnp.int32, (own_rows, count), 0) + first_row
    causal = row >= lax.broadcasted_iota(jnp.int32, (own_rows, count), 1)

    def project(source, k):
        for fetch in fetches[k]:
            fetch.wait()
        return jnp.dot(source, table[k], preferred_element_type=jnp.float32).astype(jnp.bfloat16)

    keys, values = project(normed[...], 1), project(normed[...], 2)
    queries = project(normed[pl.ds(first_row, own_rows), :], 0)
    queries_out[...] = queries
    for n in range(heads):
        at = slice(n * HD, (n + 1) * HD)
        scores = lax.dot_general(
            queries[:, at],
            keys[:, at],
            (((1,), (1,)), ((), ())),
            preferred_element_type=jnp.float32,
        )
        scores = jnp.where(causal, scores, 0.0).astype(jnp.bfloat16)
        inside_out[:, at] = jnp.dot(scores, values[:, at], preferred_element_type=jnp.float32)


def inside_block(normed, weight, own_rows):
    count, width = normed.shape
    half = weight.shape[2]
    local = pl.BlockSpec(memory_space=pltpu.VMEM)
    return pl.pallas_call(
        inside_kernel,
        in_specs=[local, pl.BlockSpec(memory_space=pl.ANY)],
        out_specs=[local] * 2,
        out_shape=[
            pltpu.VMEM((own_rows, half), jnp.bfloat16),
            pltpu.VMEM((own_rows, half), jnp.float32),
        ],
        scratch_shapes=[
            pltpu.VMEM((3, width, half), jnp.bfloat16),
            pltpu.SemaphoreType.DMA((3, 2)),
        ],
        compiler_params=pltpu.CompilerParams(vmem_limit_bytes=24 * MIB),
        cost_estimate=pl.CostEstimate(
            flops=5 * count * width * half + 4 * own_rows * count * half,
            bytes_accessed=4 * count * width,
            transcendentals=0,
        ),
        name="inside_block",
    )(in_vmem(normed), in_hbm(weight))


def heads_through(queries, inside, state, first, weight):
    own_rows, half = queries.shape
    position = lax.broadcasted_iota(jnp.int32, (own_rows, HD), 0) + first
    unit = 1.0 / (position.astype(jnp.float32) * math.sqrt(HD))
    mixed = []
    for n in range(half // HD):
        at = slice(n * HD, (n + 1) * HD)
        carried = jnp.dot(queries[:, at], state[at, :], preferred_element_type=jnp.float32)
        mixed.append(((inside[:, at] + carried) * unit).astype(jnp.bfloat16))
    return lambda: jnp.dot(
        jnp.concatenate(mixed, axis=1), weight[...], preferred_element_type=jnp.float32
    )


def first_position(own_rows):
    places = lax.axis_index(SEQ) * lax.axis_size("head") + lax.axis_index("head")
    return places * own_rows + 1


def mix_own_kernel(queries, inside, state, out_weight, series, total, weight_in, rows_in, sems):
    own_rows = queries.shape[0]
    first_row = pl.multiple_of(lax.axis_index("head") * own_rows, own_rows)
    fetches = [
        in_parts(out_weight, weight_in, sems.at[0], 2),
        in_parts(series.at[pl.ds(first_row, own_rows)], rows_in, sems.at[1], 2),
    ]
    for some in fetches:
        for fetch in some:
            fetch.start()
    through = heads_through(queries, inside, state, first_position(own_rows), weight_in)
    for some in fetches:
        for fetch in some:
            fetch.wait()
    total[...] = through() + rows_in[...].astype(jnp.float32)


def mix_own(part, state, out_weight, series):
    queries, inside = part
    own_rows, half = queries.shape
    width = series.shape[1]
    anywhere = pl.BlockSpec(memory_space=pl.ANY)
    local = pl.BlockSpec(memory_space=pltpu.VMEM)
    return pl.pallas_call(
        mix_own_kernel,
        in_specs=[local] * 3 + [anywhere] * 2,
        out_specs=local,
        out_shape=pltpu.VMEM((own_rows, width), jnp.float32),
        scratch_shapes=[
            pltpu.VMEM((half, width), jnp.bfloat16),
            pltpu.VMEM((own_rows, width), jnp.bfloat16),
            pltpu.SemaphoreType.DMA((2, 2)),
        ],
        compiler_params=pltpu.CompilerParams(vmem_limit_bytes=16 * MIB),
        cost_estimate=pl.CostEstimate(
            flops=2 * own_rows * half * (width + HD),
            bytes_accessed=8 * own_rows * width,
            transcendentals=0,
        ),
        name="mix_own",
    )(in_vmem(queries), in_vmem(inside), state, in_hbm(out_weight), in_hbm(series))


def mix_kernel(
    queries,
    inside,
    state,
    begun,
    out_weight,
    gain,
    slots,
    ids,
    router,
    slot_column,
    residual_out,
    send_out,
    weight_in,
    router_in,
    sems,
):
    own_rows, width = begun.shape
    fetches = in_parts(out_weight, weight_in, sems.at[0], 2)
    fetch_router = pltpu.make_async_copy(router, router_in, sems.at[1, 0])
    for fetch in fetches:
        fetch.start()
    fetch_router.start()
    slot = lax.broadcasted_iota(jnp.int32, (send_out.shape[0], own_rows), 0)
    chosen = jnp.where(slot == slots[...], 1.0, 0.0).astype(jnp.bfloat16)
    through = heads_through(queries, inside, state, first_position(own_rows), weight_in)
    for fetch in fetches:
        fetch.wait()
    total = begun[...] + through()
    residual_out[:, :width] = total
    normed = normed_rows(total, gain[...]).astype(jnp.bfloat16)
    send_out[...] = jnp.dot(chosen, normed, preferred_element_type=jnp.float32).astype(
        jnp.bfloat16
    )
    fetch_router.wait()
    logits = jnp.dot(normed, router_in[...], preferred_element_type=jnp.float32)
    expert = lax.broadcasted_iota(jnp.int32, logits.shape, 1)
    logit = jnp.sum(jnp.where(expert == ids[...], logits, 0.0), axis=1, keepdims=True)
    residual_out[:, width:] = jnp.broadcast_to(jax.nn.sigmoid(logit), (own_rows, HD))


def mix_heads(part, state, begun, out_weight, gain, slots, ids, router, slot_column, slot_count):
    own_rows, width = begun.shape
    anywhere = pl.BlockSpec(memory_space=pl.ANY)
    local = pl.BlockSpec(memory_space=pltpu.VMEM)
    return pl.pallas_call(
        mix_kernel,
        in_specs=[local] * 4 + [anywhere] + [local] * 3 + [anywhere] * 2,
        out_specs=[local] * 2,
        out_shape=[
            pltpu.VMEM((own_rows, width + HD), jnp.float32),
            jax.ShapeDtypeStruct((slot_count, width), jnp.bfloat16),
        ],
        scratch_shapes=[
            pltpu.VMEM(out_weight.shape, jnp.bfloat16),
            pltpu.VMEM(router.shape, jnp.bfloat16),
            pltpu.SemaphoreType.DMA((2, 2)),
        ],
        compiler_params=pltpu.CompilerParams(vmem_limit_bytes=24 * MIB),
        cost_estimate=pl.CostEstimate(
            flops=2 * own_rows * width * (width + 2 * HD + slot_count),
            bytes_accessed=12 * own_rows * width,
            transcendentals=own_rows,
        ),
        name="mix_heads",
    )(
        *(in_vmem(array) for array in part),
        state,
        in_vmem(begun),
        in_hbm(out_weight),
        gain,
        slots,
        ids,
        in_hbm(router),
        slot_column,
    )


def combine_kernel(returned, residual, slots, out, held, sems):
    own_rows, width = held.shape
    parts = 4
    leave = in_parts(held, out, sems, parts)
    slot = lax.broadcasted_iota(jnp.int32, (own_rows, returned.shape[0]), 1)
    chosen = jnp.where(slot == slots[...], 1.0, 0.0).astype(jnp.bfloat16)
    size = own_rows // parts
    for k in range(parts):
        at = slice(k * size, (k + 1) * size)
        routed = jnp.dot(chosen[at], returned[...], preferred_element_type=jnp.float32)
        weight = jnp.concatenate([residual[at, width:]] * (width // HD), axis=1)
        held[at, :] = (residual[at, :width] + weight * routed).astype(jnp.bfloat16)
        leave[k].start()
    for copy in leave:
        copy.wait()


def combine(returned, residual, slots):
    own_rows, width = residual.shape[0], returned.shape[1]
    anywhere = pl.BlockSpec(memory_space=pl.ANY)
    local = pl.BlockSpec(memory_space=pltpu.VMEM)
    return pl.pallas_call(
        combine_kernel,
        in_specs=[local] * 3,
        out_specs=anywhere,
        out_shape=pltpu.HBM((own_rows, width), jnp.bfloat16),
        scratch_shapes=[
            pltpu.VMEM((own_rows, width), jnp.bfloat16),
            pltpu.SemaphoreType.DMA((4,)),
        ],
        compiler_params=pltpu.CompilerParams(vmem_limit_bytes=24 * MIB),
        cost_estimate=pl.CostEstimate(
            flops=2 * own_rows * width * returned.shape[0],
            bytes_accessed=10 * own_rows * width,
            transcendentals=0,
        ),
        name="combine",
    )(returned, in_vmem(residual), slots)


def on_device(
    series,
    norm_attn,
    qkv_weight,
    out_weight,
    norm_moe,
    router_weight,
    expert_ids,
    gate_weight,
    up_weight,
    down_weight,
):
    width = series.shape[2]
    head_count = lax.axis_size("head")
    seq_size = lax.axis_size(SEQ)
    own_rows = series.shape[1] // head_count

    qkv_own = jnp.moveaxis(qkv_weight, 1, 0)
    own_expert = (gate_weight[0], up_weight[0], down_weight[0])
    qkv_other = from_partner(qkv_own)
    out_other = from_partner(out_weight)
    other_expert = tuple(from_partner(w) for w in own_expert)

    state, normed_in = block_state(series[0], qkv_own, norm_attn)
    pieces = exchange(state.reshape(seq_size, state.shape[0] // seq_size, HD), SEQ)
    state_own = exchange(prefix(pieces), SEQ)
    state_other = from_partner(state_own)
    part_own = inside_block(normed_in, qkv_own, own_rows)
    part_other = inside_block(normed_in, qkv_other, own_rows)

    route_ids = expert_ids[0, :, 0]
    expert_count = router_weight.shape[1]
    capacity = 2 * own_rows // expert_count
    earlier_row = jnp.arange(own_rows)[None, :] < jnp.arange(own_rows)[:, None]
    same_expert = route_ids[:, None] == route_ids[None, :]
    slot_rank = jnp.sum(jnp.logical_and(same_expert, earlier_row), axis=1)
    slot_index = route_ids * capacity + slot_rank
    slots = slot_index[None, :]
    slot_column = slot_index[:, None]

    begun = mix_own(part_own, state_own.reshape(state.shape), out_weight, series[0])
    residual, send_buffer = mix_heads(
        part_other,
        state_other.reshape(state.shape),
        begun,
        out_other,
        norm_moe,
        slots,
        route_ids[:, None],
        router_weight,
        slot_column,
        expert_count * capacity,
    )
    received = exchange(send_buffer.reshape(expert_count, capacity, width), SEQ_DP)

    expert_out = expert_of(received.reshape(-1, width), own_expert, other_expert)
    returned = exchange(expert_out.reshape(received.shape), SEQ_DP)
    layer_out = combine(returned.reshape(send_buffer.shape), residual, slot_column)
    return layer_out[None]


def solution(mesh):
    split = Mesh(
        mesh.devices.reshape(8, 4, mesh.shape["head"], mesh.shape["dp"]),
        ("seq_0", "seq_1", "head", "dp"),
    )
    placed = (
        P("dp", SEQ, None),
        P(),
        P(None, None, "head"),
        P("head", None),
        P(),
        P(),
        P("dp", SEQ_HEAD, None),
        P(SEQ_DP, None, "head"),
        P(SEQ_DP, None, "head"),
        P(SEQ_DP, "head", None),
    )

    return jax.shard_map(
        on_device, mesh=split, in_specs=placed, out_specs=P("dp", SEQ_HEAD, None), check_vma=False
    )
```

```python
import math

import jax
import jax.numpy as jnp
from jax import lax
from jax.experimental import pallas as pl
from jax.experimental.pallas import tpu as pltpu
from jax.sharding import Mesh
from jax.sharding import PartitionSpec as P


HD = 128
SEQ = ("seq_0", "seq_1")
SEQ_DP = ("seq_0", "seq_1", "dp")
SEQ_HEAD = ("seq_0", "seq_1", "head")
NORM_EPS = 1e-06
FF_BLOCK = 512
MIB = 1024 * 1024


def from_partner(shard):
    return lax.ppermute(shard, "head", [(0, 1), (1, 0)])


def exchange(pieces, axes):
    return lax.all_to_all(pieces, axes, split_axis=0, concat_axis=0, tiled=True)


def expert_kernel(rows, gate_a, up_a, down_a, gate_b, up_b, down_b, out, gate, up, down, total, sems):
    blocks = gate.shape[0]
    own_blocks = blocks // 2
    first = FF_BLOCK // 2

    def copies(k):
        gates, ups, downs = (gate_a, up_a, down_a) if k < own_blocks else (gate_b, up_b, down_b)
        base = (k % own_blocks) * FF_BLOCK
        spans = ((0, first), (first, first)) if k == 0 else ((0, FF_BLOCK),)
        for n, (at, size) in enumerate(spans):
            row = 0 if k == 0 and n == 0 else k + 1
            to, source = pl.ds(at, size), pl.ds(base + at, size)
            yield pltpu.make_async_copy(gates.at[:, source], gate.at[k, :, to], sems.at[row, 0])
            yield pltpu.make_async_copy(ups.at[:, source], up.at[k, :, to], sems.at[row, 1])
            yield pltpu.make_async_copy(downs.at[source, :], down.at[k, to, :], sems.at[row, 2])

    started = [list(copies(k)) for k in range(blocks)]
    for some in started:
        for copy in some:
            copy.start()

    def part(gates, ups, downs):
        x = rows[...]
        g = jnp.dot(x, gates, preferred_element_type=jnp.float32)
        u = jnp.dot(x, ups, preferred_element_type=jnp.float32)
        hidden = (g * (0.5 + 0.5 * jnp.tanh(0.5 * g)) * u).astype(jnp.bfloat16)
        return jnp.dot(hidden, downs, preferred_element_type=jnp.float32)

    for copy in started[0][:3]:
        copy.wait()
    total[...] = part(gate[0, :, :first], up[0, :, :first], down[0, :first, :])
    for copy in started[0][3:]:
        copy.wait()
    total[...] += part(gate[0, :, first:], up[0, :, first:], down[0, first:, :])

    def step(k, carry):
        whole = pl.ds(0, FF_BLOCK)
        pltpu.make_async_copy(gate_a.at[:, whole], gate.at[k], sems.at[k + 1, 0]).wait()
        pltpu.make_async_copy(up_a.at[:, whole], up.at[k], sems.at[k + 1, 1]).wait()
        pltpu.make_async_copy(down_a.at[whole, :], down.at[k], sems.at[k + 1, 2]).wait()
        total[...] += part(gate[k], up[k], down[k])
        return carry

    lax.fori_loop(1, blocks, step, 0)
    out[...] = total[...].astype(out.dtype)


def expert_of(rows, own, partner):
    count, width = rows.shape
    units = own[0].shape[1]
    blocks = 2 * units // FF_BLOCK
    local = pl.BlockSpec(memory_space=pltpu.VMEM)
    return pl.pallas_call(
        expert_kernel,
        in_specs=[local] + [pl.BlockSpec(memory_space=pl.ANY)] * 6,
        out_specs=local,
        out_shape=jax.ShapeDtypeStruct((count, width), jnp.bfloat16),
        scratch_shapes=[
            pltpu.VMEM((blocks, width, FF_BLOCK), jnp.bfloat16),
            pltpu.VMEM((blocks, width, FF_BLOCK), jnp.bfloat16),
            pltpu.VMEM((blocks, FF_BLOCK, width), jnp.bfloat16),
            pltpu.VMEM((count, width), jnp.float32),
            pltpu.SemaphoreType.DMA((blocks + 1, 3)),
        ],
        compiler_params=pltpu.CompilerParams(vmem_limit_bytes=36 * MIB),
        cost_estimate=pl.CostEstimate(
            flops=2 * count * width * units * 6,
            bytes_accessed=12 * width * units,
            transcendentals=2 * count * units,
        ),
        name="expert_mlp",
    )(rows, *(in_hbm(w) for w in own), *(in_hbm(w) for w in partner))


def in_parts(source, target, sems, parts):
    size = source.shape[0] // parts
    return [
        pltpu.make_async_copy(
            source.at[pl.ds(k * size, size)], target.at[pl.ds(k * size, size)], sems.at[k]
        )
        for k in range(parts)
    ]


def in_hbm(array):
    return pltpu.with_memory_space_constraint(array, pltpu.HBM)


def in_vmem(array):
    return pltpu.with_memory_space_constraint(array, pltpu.VMEM)


def normed_rows(rows, gain):
    x = rows.astype(jnp.float32)
    mean = jnp.sum(x * x, axis=-1, keepdims=True) * (1.0 / x.shape[1])
    return x * lax.rsqrt(mean + NORM_EPS) * gain.reshape(1, -1)


def state_kernel(series, weight, gain, state_out, normed_out, rows, table, gain_in, sems):
    half = weight.shape[2]
    fetches = [in_parts(series, rows, sems.at[0], 4)] + [
        in_parts(weight.at[k], table.at[:, pl.ds((k - 1) * half, half)], sems.at[k], 4)
        for k in (1, 2)
    ]
    fetch_gain = pltpu.make_async_copy(gain, gain_in, sems.at[3, 0])
    for fetch in fetches[0]:
        fetch.start()
    fetch_gain.start()
    for some in fetches[1:]:
        for fetch in some:
            fetch.start()
    fetch_gain.wait()
    size = rows.shape[0] // len(fetches[0])
    for k, fetch in enumerate(fetches[0]):
        at = slice(k * size, (k + 1) * size)
        fetch.wait()
        normed_out[at, :] = normed_rows(rows[at, :], gain_in[...]).astype(jnp.bfloat16)
    for some in fetches[1:]:
        for fetch in some:
            fetch.wait()
    both = jnp.dot(normed_out[...], table[...], preferred_element_type=jnp.float32)
    both = both.astype(jnp.bfloat16)
    heads = half // HD
    for n in range(heads):
        at = slice(n * HD, (n + 1) * HD)
        state_out[at, :] = lax.dot_general(
            both[:, n * HD : (n + 1) * HD],
            both[:, half + n * HD : half + (n + 1) * HD],
            (((0,), (0,)), ((), ())),
            preferred_element_type=jnp.float32,
        ).astype(jnp.bfloat16)
    state_out[heads * HD :, :] = jnp.zeros((HD, HD), jnp.bfloat16)


def block_state(series, weight, gain):
    count, width = series.shape
    half = weight.shape[2]
    return pl.pallas_call(
        state_kernel,
        in_specs=[
            pl.BlockSpec(memory_space=pl.ANY),
            pl.BlockSpec(memory_space=pl.ANY),
            pl.BlockSpec(memory_space=pl.ANY),
        ],
        out_specs=[pl.BlockSpec(memory_space=pltpu.VMEM)] * 2,
        out_shape=[
            jax.ShapeDtypeStruct((half + HD, HD), jnp.bfloat16),
            pltpu.VMEM((count, width), jnp.bfloat16),
        ],
        scratch_shapes=[
            pltpu.VMEM((count, width), jnp.bfloat16),
            pltpu.VMEM((width, 2 * half), jnp.bfloat16),
            pltpu.VMEM((width,), jnp.float32),
            pltpu.SemaphoreType.DMA((4, 4)),
        ],
        compiler_params=pltpu.CompilerParams(vmem_limit_bytes=24 * MIB),
        cost_estimate=pl.CostEstimate(
            flops=4 * count * width * half, bytes_accessed=4 * count * width, transcendentals=count
        ),
        name="block_state",
    )(in_hbm(series), in_hbm(weight), in_hbm(gain))


def prefix_kernel(pieces, out):
    total = jnp.zeros(pieces.shape[1:], jnp.float32)
    for k in range(pieces.shape[0]):
        rounded = total.astype(jnp.bfloat16)
        out[k] = rounded
        total = total + pieces[k].astype(jnp.float32)


def prefix(pieces):
    count, lines, lanes = pieces.shape
    return pl.pallas_call(
        prefix_kernel,
        in_specs=[pl.BlockSpec(memory_space=pltpu.VMEM)],
        out_specs=pl.BlockSpec(memory_space=pltpu.VMEM),
        out_shape=jax.ShapeDtypeStruct((count, lines, lanes), jnp.bfloat16),
        compiler_params=pltpu.CompilerParams(vmem_limit_bytes=4 * MIB),
        cost_estimate=pl.CostEstimate(
            flops=count * lines * lanes, bytes_accessed=6 * count * lines * lanes, transcendentals=0
        ),
        name="prefix",
    )(pieces)


def inside_kernel(normed, weight, queries_out, inside_out, table, query_table, sems):
    count, _ = normed.shape
    own_rows, half = queries_out.shape
    heads = half // HD
    fetches = [in_parts(weight.at[0], query_table, sems.at[0], 2)] + [
        in_parts(weight.at[k], table.at[:, pl.ds((k - 1) * half, half)], sems.at[k], 2)
        for k in (1, 2)
    ]
    for some in fetches:
        for fetch in some:
            fetch.start()
    first_row = pl.multiple_of(lax.axis_index("head") * own_rows, own_rows)
    row = lax.broadcasted_iota(jnp.int32, (own_rows, count), 0) + first_row
    causal = row >= lax.broadcasted_iota(jnp.int32, (own_rows, count), 1)
    for fetch in fetches[0]:
        fetch.wait()
    queries = jnp.dot(
        normed[pl.ds(first_row, own_rows), :], query_table[...], preferred_element_type=jnp.float32
    ).astype(jnp.bfloat16)
    queries_out[...] = queries
    for some in fetches[1:]:
        for fetch in some:
            fetch.wait()
    both = jnp.dot(normed[...], table[...], preferred_element_type=jnp.float32)
    both = both.astype(jnp.bfloat16)
    for n in range(heads):
        at = slice(n * HD, (n + 1) * HD)
        scores = lax.dot_general(
            queries[:, at],
            both[:, at],
            (((1,), (1,)), ((), ())),
            preferred_element_type=jnp.float32,
        )
        scores = jnp.where(causal, scores, 0.0).astype(jnp.bfloat16)
        values = both[:, half + n * HD : half + (n + 1) * HD]
        inside_out[:, at] = jnp.dot(scores, values, preferred_element_type=jnp.float32)


def inside_block(normed, weight, own_rows):
    count, width = normed.shape
    half = weight.shape[2]
    local = pl.BlockSpec(memory_space=pltpu.VMEM)
    return pl.pallas_call(
        inside_kernel,
        in_specs=[local, pl.BlockSpec(memory_space=pl.ANY)],
        out_specs=[local] * 2,
        out_shape=[
            pltpu.VMEM((own_rows, half), jnp.bfloat16),
            pltpu.VMEM((own_rows, half), jnp.float32),
        ],
        scratch_shapes=[
            pltpu.VMEM((width, 2 * half), jnp.bfloat16),
            pltpu.VMEM((width, half), jnp.bfloat16),
            pltpu.SemaphoreType.DMA((3, 2)),
        ],
        compiler_params=pltpu.CompilerParams(vmem_limit_bytes=24 * MIB),
        cost_estimate=pl.CostEstimate(
            flops=5 * count * width * half + 4 * own_rows * count * half,
            bytes_accessed=4 * count * width,
            transcendentals=0,
        ),
        name="inside_block",
    )(in_vmem(normed), in_hbm(weight))


def heads_through(queries, inside, state, first, weight):
    own_rows, half = queries.shape
    position = lax.broadcasted_iota(jnp.int32, (own_rows, HD), 0) + first
    unit = 1.0 / (position.astype(jnp.float32) * math.sqrt(HD))
    mixed = []
    for n in range(half // HD):
        at = slice(n * HD, (n + 1) * HD)
        carried = jnp.dot(queries[:, at], state[at, :], preferred_element_type=jnp.float32)
        mixed.append(((inside[:, at] + carried) * unit).astype(jnp.bfloat16))
    return lambda: jnp.dot(
        jnp.concatenate(mixed, axis=1), weight[...], preferred_element_type=jnp.float32
    )


def first_position(own_rows):
    places = lax.axis_index(SEQ) * lax.axis_size("head") + lax.axis_index("head")
    return places * own_rows + 1


def mix_own_kernel(queries, inside, state, out_weight, series, total, weight_in, rows_in, sems):
    own_rows = queries.shape[0]
    first_row = pl.multiple_of(lax.axis_index("head") * own_rows, own_rows)
    fetches = [
        in_parts(out_weight, weight_in, sems.at[0], 2),
        in_parts(series.at[pl.ds(first_row, own_rows)], rows_in, sems.at[1], 2),
    ]
    for some in fetches:
        for fetch in some:
            fetch.start()
    through = heads_through(queries, inside, state, first_position(own_rows), weight_in)
    for some in fetches:
        for fetch in some:
            fetch.wait()
    total[...] = through() + rows_in[...].astype(jnp.float32)


def mix_own(part, state, out_weight, series):
    queries, inside = part
    own_rows, half = queries.shape
    width = series.shape[1]
    anywhere = pl.BlockSpec(memory_space=pl.ANY)
    local = pl.BlockSpec(memory_space=pltpu.VMEM)
    return pl.pallas_call(
        mix_own_kernel,
        in_specs=[local] * 3 + [anywhere] * 2,
        out_specs=local,
        out_shape=pltpu.VMEM((own_rows, width), jnp.float32),
        scratch_shapes=[
            pltpu.VMEM((half, width), jnp.bfloat16),
            pltpu.VMEM((own_rows, width), jnp.bfloat16),
            pltpu.SemaphoreType.DMA((2, 2)),
        ],
        compiler_params=pltpu.CompilerParams(vmem_limit_bytes=16 * MIB),
        cost_estimate=pl.CostEstimate(
            flops=2 * own_rows * half * (width + HD),
            bytes_accessed=8 * own_rows * width,
            transcendentals=0,
        ),
        name="mix_own",
    )(in_vmem(queries), in_vmem(inside), state, in_hbm(out_weight), in_hbm(series))


def mix_kernel(
    queries,
    inside,
    state,
    begun,
    out_weight,
    gain,
    slots,
    ids,
    router,
    slot_column,
    residual_out,
    send_out,
    weight_in,
    router_in,
    sems,
):
    own_rows, width = begun.shape
    fetches = in_parts(out_weight, weight_in, sems.at[0], 2)
    fetch_router = pltpu.make_async_copy(router, router_in, sems.at[1, 0])
    for fetch in fetches:
        fetch.start()
    fetch_router.start()
    slot = lax.broadcasted_iota(jnp.int32, (send_out.shape[0], own_rows), 0)
    chosen = jnp.where(slot == slots[...], 1.0, 0.0).astype(jnp.bfloat16)
    through = heads_through(queries, inside, state, first_position(own_rows), weight_in)
    for fetch in fetches:
        fetch.wait()
    total = begun[...] + through()
    residual_out[:, :width] = total
    normed = normed_rows(total, gain[...]).astype(jnp.bfloat16)
    send_out[...] = jnp.dot(chosen, normed, preferred_element_type=jnp.float32).astype(
        jnp.bfloat16
    )
    fetch_router.wait()
    logits = jnp.dot(normed, router_in[...], preferred_element_type=jnp.float32)
    expert = lax.broadcasted_iota(jnp.int32, logits.shape, 1)
    logit = jnp.sum(jnp.where(expert == ids[...], logits, 0.0), axis=1, keepdims=True)
    residual_out[:, width:] = jnp.broadcast_to(jax.nn.sigmoid(logit), (own_rows, HD))


def mix_heads(part, state, begun, out_weight, gain, slots, ids, router, slot_column, slot_count):
    own_rows, width = begun.shape
    anywhere = pl.BlockSpec(memory_space=pl.ANY)
    local = pl.BlockSpec(memory_space=pltpu.VMEM)
    return pl.pallas_call(
        mix_kernel,
        in_specs=[local] * 4 + [anywhere] + [local] * 3 + [anywhere] * 2,
        out_specs=[local] * 2,
        out_shape=[
            pltpu.VMEM((own_rows, width + HD), jnp.float32),
            jax.ShapeDtypeStruct((slot_count, width), jnp.bfloat16),
        ],
        scratch_shapes=[
            pltpu.VMEM(out_weight.shape, jnp.bfloat16),
            pltpu.VMEM(router.shape, jnp.bfloat16),
            pltpu.SemaphoreType.DMA((2, 2)),
        ],
        compiler_params=pltpu.CompilerParams(vmem_limit_bytes=24 * MIB),
        cost_estimate=pl.CostEstimate(
            flops=2 * own_rows * width * (width + 2 * HD + slot_count),
            bytes_accessed=12 * own_rows * width,
            transcendentals=own_rows,
        ),
        name="mix_heads",
    )(
        *(in_vmem(array) for array in part),
        state,
        in_vmem(begun),
        in_hbm(out_weight),
        gain,
        slots,
        ids,
        in_hbm(router),
        slot_column,
    )


def combine_kernel(returned, residual, slots, out, held, sems):
    own_rows, width = held.shape
    parts = 4
    leave = in_parts(held, out, sems, parts)
    slot = lax.broadcasted_iota(jnp.int32, (own_rows, returned.shape[0]), 1)
    chosen = jnp.where(slot == slots[...], 1.0, 0.0).astype(jnp.bfloat16)
    size = own_rows // parts
    for k in range(parts):
        at = slice(k * size, (k + 1) * size)
        routed = jnp.dot(chosen[at], returned[...], preferred_element_type=jnp.float32)
        weight = jnp.concatenate([residual[at, width:]] * (width // HD), axis=1)
        held[at, :] = (residual[at, :width] + weight * routed).astype(jnp.bfloat16)
        leave[k].start()
    for copy in leave:
        copy.wait()


def combine(returned, residual, slots):
    own_rows, width = residual.shape[0], returned.shape[1]
    anywhere = pl.BlockSpec(memory_space=pl.ANY)
    local = pl.BlockSpec(memory_space=pltpu.VMEM)
    return pl.pallas_call(
        combine_kernel,
        in_specs=[local] * 3,
        out_specs=anywhere,
        out_shape=pltpu.HBM((own_rows, width), jnp.bfloat16),
        scratch_shapes=[
            pltpu.VMEM((own_rows, width), jnp.bfloat16),
            pltpu.SemaphoreType.DMA((4,)),
        ],
        compiler_params=pltpu.CompilerParams(vmem_limit_bytes=24 * MIB),
        cost_estimate=pl.CostEstimate(
            flops=2 * own_rows * width * returned.shape[0],
            bytes_accessed=10 * own_rows * width,
            transcendentals=0,
        ),
        name="combine",
    )(returned, in_vmem(residual), slots)


def on_device(
    series,
    norm_attn,
    qkv_weight,
    out_weight,
    norm_moe,
    router_weight,
    expert_ids,
    gate_weight,
    up_weight,
    down_weight,
):
    width = series.shape[2]
    head_count = lax.axis_size("head")
    seq_size = lax.axis_size(SEQ)
    own_rows = series.shape[1] // head_count

    qkv_own = jnp.moveaxis(qkv_weight, 1, 0)
    own_expert = (gate_weight[0], up_weight[0], down_weight[0])
    qkv_other = from_partner(qkv_own)
    out_other = from_partner(out_weight)
    gate_other, up_other = (from_partner(w) for w in own_expert[:2])
    down_other = from_partner(own_expert[2])
    other_expert = (gate_other, up_other, down_other)

    state, normed_in = block_state(series[0], qkv_own, norm_attn)
    pieces = exchange(state.reshape(seq_size, state.shape[0] // seq_size, HD), SEQ)
    state_own = exchange(prefix(pieces), SEQ)
    state_other = from_partner(state_own)
    part_own = inside_block(normed_in, qkv_own, own_rows)
    part_other = inside_block(normed_in, qkv_other, own_rows)

    route_ids = expert_ids[0, :, 0]
    expert_count = router_weight.shape[1]
    capacity = 2 * own_rows // expert_count
    earlier_row = jnp.arange(own_rows)[None, :] < jnp.arange(own_rows)[:, None]
    same_expert = route_ids[:, None] == route_ids[None, :]
    slot_rank = jnp.sum(jnp.logical_and(same_expert, earlier_row), axis=1)
    slot_index = route_ids * capacity + slot_rank
    slots = slot_index[None, :]
    slot_column = slot_index[:, None]

    begun = mix_own(part_own, state_own.reshape(state.shape), out_weight, series[0])
    residual, send_buffer = mix_heads(
        part_other,
        state_other.reshape(state.shape),
        begun,
        out_other,
        norm_moe,
        slots,
        route_ids[:, None],
        router_weight,
        slot_column,
        expert_count * capacity,
    )
    received = exchange(send_buffer.reshape(expert_count, capacity, width), SEQ_DP)

    expert_out = expert_of(received.reshape(-1, width), own_expert, other_expert)
    returned = exchange(expert_out.reshape(received.shape), SEQ_DP)
    layer_out = combine(returned.reshape(send_buffer.shape), residual, slot_column)
    return layer_out[None]


def solution(mesh):
    split = Mesh(
        mesh.devices.reshape(8, 4, mesh.shape["head"], mesh.shape["dp"]),
        ("seq_0", "seq_1", "head", "dp"),
    )
    placed = (
        P("dp", SEQ, None),
        P(),
        P(None, None, "head"),
        P("head", None),
        P(),
        P(),
        P("dp", SEQ_HEAD, None),
        P(SEQ_DP, None, "head"),
        P(SEQ_DP, None, "head"),
        P(SEQ_DP, "head", None),
    )

    return jax.shard_map(
        on_device, mesh=split, in_specs=placed, out_specs=P("dp", SEQ_HEAD, None), check_vma=False
    )
```

```python
import math

import jax
import jax.numpy as jnp
from jax import lax
from jax.experimental import pallas as pl
from jax.experimental.pallas import tpu as pltpu
from jax.sharding import Mesh
from jax.sharding import PartitionSpec as P


HD = 128
SEQ = ("seq_0", "seq_1")
SEQ_DP = ("seq_0", "seq_1", "dp")
SEQ_HEAD = ("seq_0", "seq_1", "head")
NORM_EPS = 1e-06
FF_BLOCK = 1536
FF_FIRST = 512
MIB = 1024 * 1024


def from_partner(shard):
    return lax.ppermute(shard, "head", [(0, 1), (1, 0)])


def exchange(pieces, axes):
    return lax.all_to_all(pieces, axes, split_axis=0, concat_axis=0, tiled=True)


def expert_kernel(rows, gate_a, up_a, down_a, gate_b, up_b, down_b, out, gate, up, down, total, sems):
    blocks = gate.shape[0]
    own_blocks = blocks // 2
    first = FF_FIRST

    def copies(k):
        gates, ups, downs = (gate_a, up_a, down_a) if k < own_blocks else (gate_b, up_b, down_b)
        base = (k % own_blocks) * FF_BLOCK
        spans = ((0, first), (first, FF_BLOCK - first)) if k == 0 else ((0, FF_BLOCK),)
        for n, (at, size) in enumerate(spans):
            row = 0 if k == 0 and n == 0 else k + 1
            to, source = pl.ds(at, size), pl.ds(base + at, size)
            yield pltpu.make_async_copy(gates.at[:, source], gate.at[k, :, to], sems.at[row, 0])
            yield pltpu.make_async_copy(ups.at[:, source], up.at[k, :, to], sems.at[row, 1])
            yield pltpu.make_async_copy(downs.at[source, :], down.at[k, to, :], sems.at[row, 2])

    started = [list(copies(k)) for k in range(blocks)]
    for some in started:
        for copy in some:
            copy.start()

    def part(gates, ups, downs):
        x = rows[...]
        g = jnp.dot(x, gates, preferred_element_type=jnp.float32)
        u = jnp.dot(x, ups, preferred_element_type=jnp.float32)
        hidden = (g * (0.5 + 0.5 * jnp.tanh(0.5 * g)) * u).astype(jnp.bfloat16)
        return jnp.dot(hidden, downs, preferred_element_type=jnp.float32)

    for copy in started[0][:3]:
        copy.wait()
    total[...] = part(gate[0, :, :first], up[0, :, :first], down[0, :first, :])
    for copy in started[0][3:]:
        copy.wait()
    total[...] += part(gate[0, :, first:], up[0, :, first:], down[0, first:, :])

    def step(k, carry):
        whole = pl.ds(0, FF_BLOCK)
        pltpu.make_async_copy(gate_a.at[:, whole], gate.at[k], sems.at[k + 1, 0]).wait()
        pltpu.make_async_copy(up_a.at[:, whole], up.at[k], sems.at[k + 1, 1]).wait()
        pltpu.make_async_copy(down_a.at[whole, :], down.at[k], sems.at[k + 1, 2]).wait()
        total[...] += part(gate[k], up[k], down[k])
        return carry

    lax.fori_loop(1, blocks, step, 0)
    out[...] = total[...].astype(out.dtype)


def expert_of(rows, own, partner):
    count, width = rows.shape
    units = own[0].shape[1]
    blocks = 2 * units // FF_BLOCK
    local = pl.BlockSpec(memory_space=pltpu.VMEM)
    return pl.pallas_call(
        expert_kernel,
        in_specs=[local] + [pl.BlockSpec(memory_space=pl.ANY)] * 6,
        out_specs=local,
        out_shape=jax.ShapeDtypeStruct((count, width), jnp.bfloat16),
        scratch_shapes=[
            pltpu.VMEM((blocks, width, FF_BLOCK), jnp.bfloat16),
            pltpu.VMEM((blocks, width, FF_BLOCK), jnp.bfloat16),
            pltpu.VMEM((blocks, FF_BLOCK, width), jnp.bfloat16),
            pltpu.VMEM((count, width), jnp.float32),
            pltpu.SemaphoreType.DMA((blocks + 1, 3)),
        ],
        compiler_params=pltpu.CompilerParams(vmem_limit_bytes=36 * MIB),
        cost_estimate=pl.CostEstimate(
            flops=2 * count * width * units * 6,
            bytes_accessed=12 * width * units,
            transcendentals=2 * count * units,
        ),
        name="expert_mlp",
    )(rows, *(in_hbm(w) for w in own), *(in_hbm(w) for w in partner))


def in_parts(source, target, sems, parts):
    size = source.shape[0] // parts
    return [
        pltpu.make_async_copy(
            source.at[pl.ds(k * size, size)], target.at[pl.ds(k * size, size)], sems.at[k]
        )
        for k in range(parts)
    ]


def in_hbm(array):
    return pltpu.with_memory_space_constraint(array, pltpu.HBM)


def in_vmem(array):
    return pltpu.with_memory_space_constraint(array, pltpu.VMEM)


def normed_rows(rows, gain):
    x = rows.astype(jnp.float32)
    mean = jnp.sum(x * x, axis=-1, keepdims=True) * (1.0 / x.shape[1])
    return x * lax.rsqrt(mean + NORM_EPS) * gain.reshape(1, -1)


def state_kernel(series, weight, gain, state_out, normed_out, rows, table, gain_in, sems):
    half = weight.shape[2]
    fetches = [in_parts(series, rows, sems.at[0], 4)] + [
        in_parts(weight.at[k], table.at[:, pl.ds((k - 1) * half, half)], sems.at[k], 4)
        for k in (1, 2)
    ]
    fetch_gain = pltpu.make_async_copy(gain, gain_in, sems.at[3, 0])
    for fetch in fetches[0]:
        fetch.start()
    fetch_gain.start()
    for some in fetches[1:]:
        for fetch in some:
            fetch.start()
    fetch_gain.wait()
    size = rows.shape[0] // len(fetches[0])
    for k, fetch in enumerate(fetches[0]):
        at = slice(k * size, (k + 1) * size)
        fetch.wait()
        normed_out[at, :] = normed_rows(rows[at, :], gain_in[...]).astype(jnp.bfloat16)
    for some in fetches[1:]:
        for fetch in some:
            fetch.wait()
    both = jnp.dot(normed_out[...], table[...], preferred_element_type=jnp.float32)
    both = both.astype(jnp.bfloat16)
    heads = half // HD
    for n in range(heads):
        at = slice(n * HD, (n + 1) * HD)
        state_out[at, :] = lax.dot_general(
            both[:, n * HD : (n + 1) * HD],
            both[:, half + n * HD : half + (n + 1) * HD],
            (((0,), (0,)), ((), ())),
            preferred_element_type=jnp.float32,
        ).astype(jnp.bfloat16)
    state_out[heads * HD :, :] = jnp.zeros((HD, HD), jnp.bfloat16)


def block_state(series, weight, gain):
    count, width = series.shape
    half = weight.shape[2]
    return pl.pallas_call(
        state_kernel,
        in_specs=[
            pl.BlockSpec(memory_space=pl.ANY),
            pl.BlockSpec(memory_space=pl.ANY),
            pl.BlockSpec(memory_space=pl.ANY),
        ],
        out_specs=[pl.BlockSpec(memory_space=pltpu.VMEM)] * 2,
        out_shape=[
            jax.ShapeDtypeStruct((half + HD, HD), jnp.bfloat16),
            pltpu.VMEM((count, width), jnp.bfloat16),
        ],
        scratch_shapes=[
            pltpu.VMEM((count, width), jnp.bfloat16),
            pltpu.VMEM((width, 2 * half), jnp.bfloat16),
            pltpu.VMEM((width,), jnp.float32),
            pltpu.SemaphoreType.DMA((4, 4)),
        ],
        compiler_params=pltpu.CompilerParams(vmem_limit_bytes=24 * MIB),
        cost_estimate=pl.CostEstimate(
            flops=4 * count * width * half, bytes_accessed=4 * count * width, transcendentals=count
        ),
        name="block_state",
    )(in_hbm(series), in_hbm(weight), in_hbm(gain))


def prefix_kernel(pieces, out):
    total = jnp.zeros(pieces.shape[1:], jnp.float32)
    for k in range(pieces.shape[0]):
        rounded = total.astype(jnp.bfloat16)
        out[k] = rounded
        total = total + pieces[k].astype(jnp.float32)


def prefix(pieces):
    count, lines, lanes = pieces.shape
    return pl.pallas_call(
        prefix_kernel,
        in_specs=[pl.BlockSpec(memory_space=pltpu.VMEM)],
        out_specs=pl.BlockSpec(memory_space=pltpu.VMEM),
        out_shape=jax.ShapeDtypeStruct((count, lines, lanes), jnp.bfloat16),
        compiler_params=pltpu.CompilerParams(vmem_limit_bytes=4 * MIB),
        cost_estimate=pl.CostEstimate(
            flops=count * lines * lanes, bytes_accessed=6 * count * lines * lanes, transcendentals=0
        ),
        name="prefix",
    )(pieces)


def inside_kernel(normed, weight, queries_out, inside_out, table, query_table, sems):
    count, _ = normed.shape
    own_rows, half = queries_out.shape
    heads = half // HD
    fetches = [in_parts(weight.at[0], query_table, sems.at[0], 2)] + [
        in_parts(weight.at[k], table.at[:, pl.ds((k - 1) * half, half)], sems.at[k], 2)
        for k in (1, 2)
    ]
    for some in fetches:
        for fetch in some:
            fetch.start()
    first_row = pl.multiple_of(lax.axis_index("head") * own_rows, own_rows)
    row = lax.broadcasted_iota(jnp.int32, (own_rows, count), 0) + first_row
    causal = row >= lax.broadcasted_iota(jnp.int32, (own_rows, count), 1)
    for fetch in fetches[0]:
        fetch.wait()
    queries = jnp.dot(
        normed[pl.ds(first_row, own_rows), :], query_table[...], preferred_element_type=jnp.float32
    ).astype(jnp.bfloat16)
    queries_out[...] = queries
    for some in fetches[1:]:
        for fetch in some:
            fetch.wait()
    both = jnp.dot(normed[...], table[...], preferred_element_type=jnp.float32)
    both = both.astype(jnp.bfloat16)
    for n in range(heads):
        at = slice(n * HD, (n + 1) * HD)
        scores = lax.dot_general(
            queries[:, at],
            both[:, at],
            (((1,), (1,)), ((), ())),
            preferred_element_type=jnp.float32,
        )
        scores = jnp.where(causal, scores, 0.0).astype(jnp.bfloat16)
        values = both[:, half + n * HD : half + (n + 1) * HD]
        inside_out[:, at] = jnp.dot(scores, values, preferred_element_type=jnp.float32)


def inside_block(normed, weight, own_rows):
    count, width = normed.shape
    half = weight.shape[2]
    local = pl.BlockSpec(memory_space=pltpu.VMEM)
    return pl.pallas_call(
        inside_kernel,
        in_specs=[local, pl.BlockSpec(memory_space=pl.ANY)],
        out_specs=[local] * 2,
        out_shape=[
            pltpu.VMEM((own_rows, half), jnp.bfloat16),
            pltpu.VMEM((own_rows, half), jnp.float32),
        ],
        scratch_shapes=[
            pltpu.VMEM((width, 2 * half), jnp.bfloat16),
            pltpu.VMEM((width, half), jnp.bfloat16),
            pltpu.SemaphoreType.DMA((3, 2)),
        ],
        compiler_params=pltpu.CompilerParams(vmem_limit_bytes=24 * MIB),
        cost_estimate=pl.CostEstimate(
            flops=5 * count * width * half + 4 * own_rows * count * half,
            bytes_accessed=4 * count * width,
            transcendentals=0,
        ),
        name="inside_block",
    )(in_vmem(normed), in_hbm(weight))


def heads_through(queries, inside, state, first, weight):
    own_rows, half = queries.shape
    position = lax.broadcasted_iota(jnp.int32, (own_rows, HD), 0) + first
    unit = 1.0 / (position.astype(jnp.float32) * math.sqrt(HD))
    mixed = []
    for n in range(half // HD):
        at = slice(n * HD, (n + 1) * HD)
        carried = jnp.dot(queries[:, at], state[at, :], preferred_element_type=jnp.float32)
        mixed.append(((inside[:, at] + carried) * unit).astype(jnp.bfloat16))
    return lambda: jnp.dot(
        jnp.concatenate(mixed, axis=1), weight[...], preferred_element_type=jnp.float32
    )


def first_position(own_rows):
    places = lax.axis_index(SEQ) * lax.axis_size("head") + lax.axis_index("head")
    return places * own_rows + 1


def mix_own_kernel(queries, inside, state, out_weight, series, total, weight_in, rows_in, sems):
    own_rows = queries.shape[0]
    first_row = pl.multiple_of(lax.axis_index("head") * own_rows, own_rows)
    fetches = [
        in_parts(out_weight, weight_in, sems.at[0], 2),
        in_parts(series.at[pl.ds(first_row, own_rows)], rows_in, sems.at[1], 2),
    ]
    for some in fetches:
        for fetch in some:
            fetch.start()
    through = heads_through(queries, inside, state, first_position(own_rows), weight_in)
    for some in fetches:
        for fetch in some:
            fetch.wait()
    total[...] = through() + rows_in[...].astype(jnp.float32)


def mix_own(part, state, out_weight, series):
    queries, inside = part
    own_rows, half = queries.shape
    width = series.shape[1]
    anywhere = pl.BlockSpec(memory_space=pl.ANY)
    local = pl.BlockSpec(memory_space=pltpu.VMEM)
    return pl.pallas_call(
        mix_own_kernel,
        in_specs=[local] * 3 + [anywhere] * 2,
        out_specs=local,
        out_shape=pltpu.VMEM((own_rows, width), jnp.float32),
        scratch_shapes=[
            pltpu.VMEM((half, width), jnp.bfloat16),
            pltpu.VMEM((own_rows, width), jnp.bfloat16),
            pltpu.SemaphoreType.DMA((2, 2)),
        ],
        compiler_params=pltpu.CompilerParams(vmem_limit_bytes=16 * MIB),
        cost_estimate=pl.CostEstimate(
            flops=2 * own_rows * half * (width + HD),
            bytes_accessed=8 * own_rows * width,
            transcendentals=0,
        ),
        name="mix_own",
    )(in_vmem(queries), in_vmem(inside), state, in_hbm(out_weight), in_hbm(series))


def mix_kernel(
    queries,
    inside,
    state,
    begun,
    out_weight,
    gain,
    slots,
    ids,
    router,
    slot_column,
    residual_out,
    send_out,
    weight_in,
    router_in,
    sems,
):
    own_rows, width = begun.shape
    fetches = in_parts(out_weight, weight_in, sems.at[0], 2)
    fetch_router = pltpu.make_async_copy(router, router_in, sems.at[1, 0])
    for fetch in fetches:
        fetch.start()
    fetch_router.start()
    slot = lax.broadcasted_iota(jnp.int32, (send_out.shape[0], own_rows), 0)
    chosen = jnp.where(slot == slots[...], 1.0, 0.0).astype(jnp.bfloat16)
    through = heads_through(queries, inside, state, first_position(own_rows), weight_in)
    for fetch in fetches:
        fetch.wait()
    total = begun[...] + through()
    residual_out[:, :width] = total
    normed = normed_rows(total, gain[...]).astype(jnp.bfloat16)
    send_out[...] = jnp.dot(chosen, normed, preferred_element_type=jnp.float32).astype(
        jnp.bfloat16
    )
    fetch_router.wait()
    logits = jnp.dot(normed, router_in[...], preferred_element_type=jnp.float32)
    expert = lax.broadcasted_iota(jnp.int32, logits.shape, 1)
    logit = jnp.sum(jnp.where(expert == ids[...], logits, 0.0), axis=1, keepdims=True)
    residual_out[:, width:] = jnp.broadcast_to(jax.nn.sigmoid(logit), (own_rows, HD))


def mix_heads(part, state, begun, out_weight, gain, slots, ids, router, slot_column, slot_count):
    own_rows, width = begun.shape
    anywhere = pl.BlockSpec(memory_space=pl.ANY)
    local = pl.BlockSpec(memory_space=pltpu.VMEM)
    return pl.pallas_call(
        mix_kernel,
        in_specs=[local] * 4 + [anywhere] + [local] * 3 + [anywhere] * 2,
        out_specs=[local] * 2,
        out_shape=[
            pltpu.VMEM((own_rows, width + HD), jnp.float32),
            jax.ShapeDtypeStruct((slot_count, width), jnp.bfloat16),
        ],
        scratch_shapes=[
            pltpu.VMEM(out_weight.shape, jnp.bfloat16),
            pltpu.VMEM(router.shape, jnp.bfloat16),
            pltpu.SemaphoreType.DMA((2, 2)),
        ],
        compiler_params=pltpu.CompilerParams(vmem_limit_bytes=24 * MIB),
        cost_estimate=pl.CostEstimate(
            flops=2 * own_rows * width * (width + 2 * HD + slot_count),
            bytes_accessed=12 * own_rows * width,
            transcendentals=own_rows,
        ),
        name="mix_heads",
    )(
        *(in_vmem(array) for array in part),
        state,
        in_vmem(begun),
        in_hbm(out_weight),
        gain,
        slots,
        ids,
        in_hbm(router),
        slot_column,
    )


def combine_kernel(returned, residual, slots, out, held, sems):
    own_rows, width = held.shape
    parts = 4
    leave = in_parts(held, out, sems, parts)
    slot = lax.broadcasted_iota(jnp.int32, (own_rows, returned.shape[0]), 1)
    chosen = jnp.where(slot == slots[...], 1.0, 0.0).astype(jnp.bfloat16)
    size = own_rows // parts
    for k in range(parts):
        at = slice(k * size, (k + 1) * size)
        routed = jnp.dot(chosen[at], returned[...], preferred_element_type=jnp.float32)
        weight = jnp.concatenate([residual[at, width:]] * (width // HD), axis=1)
        held[at, :] = (residual[at, :width] + weight * routed).astype(jnp.bfloat16)
        leave[k].start()
    for copy in leave:
        copy.wait()


def combine(returned, residual, slots):
    own_rows, width = residual.shape[0], returned.shape[1]
    anywhere = pl.BlockSpec(memory_space=pl.ANY)
    local = pl.BlockSpec(memory_space=pltpu.VMEM)
    return pl.pallas_call(
        combine_kernel,
        in_specs=[local] * 3,
        out_specs=anywhere,
        out_shape=pltpu.HBM((own_rows, width), jnp.bfloat16),
        scratch_shapes=[
            pltpu.VMEM((own_rows, width), jnp.bfloat16),
            pltpu.SemaphoreType.DMA((4,)),
        ],
        compiler_params=pltpu.CompilerParams(vmem_limit_bytes=24 * MIB),
        cost_estimate=pl.CostEstimate(
            flops=2 * own_rows * width * returned.shape[0],
            bytes_accessed=10 * own_rows * width,
            transcendentals=0,
        ),
        name="combine",
    )(returned, in_vmem(residual), slots)


def on_device(
    series,
    norm_attn,
    qkv_weight,
    out_weight,
    norm_moe,
    router_weight,
    expert_ids,
    gate_weight,
    up_weight,
    down_weight,
):
    width = series.shape[2]
    head_count = lax.axis_size("head")
    seq_size = lax.axis_size(SEQ)
    own_rows = series.shape[1] // head_count

    qkv_own = jnp.moveaxis(qkv_weight, 1, 0)
    own_expert = (gate_weight[0], up_weight[0], down_weight[0])
    qkv_other = from_partner(qkv_own)
    out_other = from_partner(out_weight)
    other_expert = tuple(from_partner(w) for w in own_expert)

    state, normed_in = block_state(series[0], qkv_own, norm_attn)
    pieces = exchange(state.reshape(seq_size, state.shape[0] // seq_size, HD), SEQ)
    state_own = exchange(prefix(pieces), SEQ)
    state_other = from_partner(state_own)
    part_own = inside_block(normed_in, qkv_own, own_rows)
    part_other = inside_block(normed_in, qkv_other, own_rows)

    route_ids = expert_ids[0, :, 0]
    expert_count = router_weight.shape[1]
    capacity = 2 * own_rows // expert_count
    earlier_row = jnp.arange(own_rows)[None, :] < jnp.arange(own_rows)[:, None]
    same_expert = route_ids[:, None] == route_ids[None, :]
    slot_rank = jnp.sum(jnp.logical_and(same_expert, earlier_row), axis=1)
    slot_index = route_ids * capacity + slot_rank
    slots = slot_index[None, :]
    slot_column = slot_index[:, None]

    begun = mix_own(part_own, state_own.reshape(state.shape), out_weight, series[0])
    residual, send_buffer = mix_heads(
        part_other,
        state_other.reshape(state.shape),
        begun,
        out_other,
        norm_moe,
        slots,
        route_ids[:, None],
        router_weight,
        slot_column,
        expert_count * capacity,
    )
    received = exchange(send_buffer.reshape(expert_count, capacity, width), SEQ_DP)

    expert_out = expert_of(received.reshape(-1, width), own_expert, other_expert)
    returned = exchange(expert_out.reshape(received.shape), SEQ_DP)
    layer_out = combine(returned.reshape(send_buffer.shape), residual, slot_column)
    return layer_out[None]


def solution(mesh):
    split = Mesh(
        mesh.devices.reshape(8, 4, mesh.shape["head"], mesh.shape["dp"]),
        ("seq_0", "seq_1", "head", "dp"),
    )
    placed = (
        P("dp", SEQ, None),
        P(),
        P(None, None, "head"),
        P("head", None),
        P(),
        P(),
        P("dp", SEQ_HEAD, None),
        P(SEQ_DP, None, "head"),
        P(SEQ_DP, None, "head"),
        P(SEQ_DP, "head", None),
    )

    return jax.shard_map(
        on_device, mesh=split, in_specs=placed, out_specs=P("dp", SEQ_HEAD, None), check_vma=False
    )
```
